256 devices in a mesh: tm: 32 (over z, x), region: 8 (over y, core).
Axes of the slice: x: 4, y: 4, z: 8, core: 2. Of those that a mesh axis runs over, the one named last changes fastest.
Arguments:
- start_primal: float32 [2048, 8, 3200], P('tm', 'region'), may hold values from 0 to 10, as said below
- demand: float32 [2048, 8, 3200], P('tm', 'region'), may hold values from -30 to 30
- unit_cost: float32 [8, 3200], P('region'), may hold values from -5 to 5
- build_cost: float32 [8, 128], P('region', 'tm'), may hold values from 0.5 to 2
- start_capacity: float32 [8, 128], P('region', 'tm'), may hold values from 0 to 2
- net_weights: float32 [8, 25, 3, 128, 128], P('region'), may hold values from -0.3125 to 0.3125
- net_columns: int32 [8, 25, 3], P('region'), may hold values from 0 to 24
- line_weights: float32 [8, 4, 128, 128], P('region'), may hold values from -0.25 to 0.25
- line_source: int32 [8, 4], replicated, may hold values from 0 to 7
- generator_map: int32 [8, 128], P('region'), may hold values from 0 to 127
Outputs:
- primal_final: float32 [2048, 8, 3200], P('tm', 'region')
- dual_final: float32 [2048, 8, 3200], P('tm', 'region')
- capacity_final: float32 [8, 128], P('region', 'tm')
The draws below stay inside these ranges and needn't reach their ends.
Inputs may be any that keep to these rules, and one draw needn't show every extreme that they name: `start_primal`: Nonnegative.
All inputs are finite; a program needn't handle non-finite values.
Results may differ from the reference program's by a relative error of at most 0.0003.
Values sent between devices are 32-bit elements; how exact they have to be, the bound alone decides.
A program may use at most 64 MiB of HBM per device.

```python
import math
import jax
import jax.numpy as jnp
from jax import lax

CB = 25
BS = 128
S = 3
NL = 4
ITERS = 4
HOURS = 2048
REGIONS = 8
NV = 3200
NI = 128


def draw_start_primal(key, part):
    keys = jax.random.split(jax.random.fold_in(key, 7), 3)
    hour_scale = 10.0 ** (0.5 * jnp.arange(HOURS, dtype=jnp.float32) / max(HOURS - 1, 1))
    column_scale = 10.0 ** jax.random.uniform(keys[0], (REGIONS, NV), jnp.float32, -0.5, 0.5)
    base = jax.random.uniform(keys[2], (HOURS, REGIONS, NV), jnp.float32, 0.0, 1.0)
    return hour_scale[:, None, None] * column_scale[None] * base


def draw_demand(key, part):
    keys = jax.random.split(jax.random.fold_in(key, 11), 5)
    hour_scale = 10.0 ** (jnp.arange(HOURS, dtype=jnp.float32) / max(HOURS - 1, 1) - 0.5)
    column_scale = 10.0 ** jax.random.uniform(keys[0], (REGIONS, NV), jnp.float32, -0.5, 0.5)
    noise = jax.random.truncated_normal(keys[4], -3.0, 3.0, (HOURS, REGIONS, NV), jnp.float32)
    return hour_scale[:, None, None] * column_scale[None] * noise


def with_ends(values, stream_key, low, top_value):
    shape = values.shape
    place = [jax.random.randint(jax.random.fold_in(stream_key, axis), (), 0, shape[axis]) for axis in range(len(shape))]
    values = values.at[tuple(place)].set(low)
    longest = shape.index(max(shape))
    place[longest] = (place[longest] + 1) % shape[longest]
    return values.at[tuple(place)].set(top_value)


def steps_of(own_key, extent, pieces, smallest, largest):
    def one(position, blocks):
        draws = jax.random.uniform(jax.random.fold_in(jax.random.fold_in(own_key, 6), position), (blocks,), jnp.float32, smallest / len(pieces), largest / len(pieces))
        return jnp.repeat(jnp.exp(draws), extent[position] // blocks).reshape((-1,) + (1,) * (len(extent) - position - 1))

    loudness = one(*pieces[0])
    for cut in pieces[1:]:
        loudness = loudness * one(*cut)
    return loudness


def bell_draw(own_key, shape, width, bound, shards=(), held_as=jnp.bfloat16):
    factor_of = steps_of(own_key, shape, shards, -0.22, 0.18) if shards else 1.0
    entries = jax.random.normal(own_key, shape, jnp.float32) * width * factor_of
    return jnp.minimum(jnp.maximum(entries, -bound), bound).astype(held_as)


def setup_inputs(seed: int = 0) -> dict:
    seeds = jax.random.split(jax.random.key(seed), 11)
    start_primal = draw_start_primal(jax.random.fold_in(seeds[10], 71), 0)
    demand = draw_demand(jax.random.fold_in(seeds[10], 71), 0)
    unit_cost = bell_draw(seeds[2], (REGIONS, NV), 1.0, 5.0, ((0, 8),), jnp.float32)
    build_cost = jnp.clip(0.5 + 1.5 * jax.random.uniform(seeds[3], (REGIONS, NI), jnp.float32) ** steps_of(seeds[3], (REGIONS, NI), ((0, 8), (1, 32)), -0.2, 0.2), 0.5, 2.0)
    start_capacity = jnp.clip(2.0 * jax.random.uniform(seeds[4], (REGIONS, NI), jnp.float32) ** steps_of(seeds[4], (REGIONS, NI), ((0, 8), (1, 32)), -0.2, 0.2), 0.0, 2.0)
    net_weights = bell_draw(seeds[5], (REGIONS, CB, S, BS, BS), (S * BS) ** -0.5, 0.3125, ((0, 8),), jnp.float32)
    net_columns = with_ends(jax.random.randint(seeds[6], (REGIONS, CB, S), 0, CB), jax.random.fold_in(seeds[6], 1), 0, CB - 1).astype(jnp.int32)
    line_weights = bell_draw(seeds[7], (REGIONS, NL, BS, BS), (NL * BS) ** -0.5, 0.25, ((0, 8),), jnp.float32)
    line_source = with_ends(jax.random.randint(seeds[8], (REGIONS, NL), 0, REGIONS), jax.random.fold_in(seeds[8], 1), 0, REGIONS - 1).astype(jnp.int32)
    generator_map = with_ends(jax.random.randint(seeds[9], (REGIONS, BS), 0, NI), jax.random.fold_in(seeds[9], 1), 0, NI - 1).astype(jnp.int32)
    return {"start_primal": start_primal, "demand": demand, "unit_cost": unit_cost, "build_cost": build_cost, "start_capacity": start_capacity, "net_weights": net_weights, "net_columns": net_columns, "line_weights": line_weights, "line_source": line_source, "generator_map": generator_map}


HIGHEST_PRECISION = lax.Precision.HIGHEST
STEP_SCALE = 0.2
EPSILON = 1e-06

def network_forward(blocks, weights, columns):
    hour_count = blocks.shape[0]
    picked = jnp.take(blocks, columns.reshape(-1), axis=1)
    flat_weights = weights.reshape(-1, weights.shape[2], weights.shape[3])
    product = jnp.einsum('hpk,pkl->hpl', picked, flat_weights, precision=HIGHEST_PRECISION)
    return product.reshape(hour_count, columns.shape[0], columns.shape[1], -1).sum(axis=2)

def network_adjoint(dual_rows, weights, columns):
    hour_count = dual_rows.shape[0]
    partial_value = jnp.einsum('hil,iskl->hisk', dual_rows, weights, precision=HIGHEST_PRECISION)
    block_count = columns.shape[0]
    placing = (columns.reshape(-1)[:, None] == jnp.arange(block_count)[None, :]).astype(jnp.float32)
    stacked = partial_value.reshape(hour_count, -1, partial_value.shape[3])
    return jnp.einsum('hpk,pc->hck', stacked, placing, precision=HIGHEST_PRECISION)

def network_regions(helper, values, weights, columns):
    moved = jnp.swapaxes(values, 0, 1)
    result = lax.map(lambda packed: helper(packed[0], packed[1], packed[2]), (moved, weights, columns))
    return jnp.swapaxes(result, 0, 1)

def reference(start_primal, demand, unit_cost, build_cost, start_capacity, net_weights, net_columns, line_weights, line_source, generator_map):
    hours_all, region_count, row_width = start_primal.shape
    block_size = net_weights.shape[3]
    block_count = row_width // block_size
    invest_count = start_capacity.shape[1]
    couple = 1.0 / math.sqrt(hours_all)
    primal_count = hours_all * region_count * row_width + region_count * invest_count
    dual_count = hours_all * region_count * row_width
    primal = start_primal.reshape(hours_all, region_count, block_count, block_size)
    target = demand.reshape(hours_all, region_count, block_count, block_size)
    dual = jnp.zeros_like(primal)
    capacity = start_capacity
    unit_rows = unit_cost.reshape(region_count, block_count, block_size)
    selector = (generator_map[:, :, None] == jnp.arange(invest_count)[None, None, :]).astype(jnp.float32)
    line_links = (line_source[:, :, None] == jnp.arange(region_count)[None, None, :]).astype(jnp.float32)
    free_column = (jnp.arange(block_count) == 3)[None, None, :, None]
    free_row = (jnp.arange(block_count) < 3)[None, None, :, None]
    primal_weight = jnp.float32(1.0)
    zero_row = jnp.zeros((1, region_count, block_size), jnp.float32)
    for iteration in range(ITERS):
        primal_step = STEP_SCALE / primal_weight
        dual_step = STEP_SCALE * primal_weight
        adjoint = network_regions(network_adjoint, dual, net_weights, net_columns)
        following = jnp.concatenate([dual[1:, :, 0], zero_row], axis=0)
        line_terms = jnp.einsum('hql,qjkl->hqjk', dual[:, :, 1], line_weights, precision=HIGHEST_PRECISION)
        line_back = jnp.einsum('hqjk,qjr->hrk', line_terms, line_links, precision=HIGHEST_PRECISION)
        adjoint = adjoint.at[:, :, 0].add(-following).at[:, :, 3].add(line_back)
        capacity_grad = couple * jnp.einsum('rg,rgm->rm', lax.optimization_barrier(jnp.sum(dual[:, :, 2], axis=0)), selector, precision=HIGHEST_PRECISION)
        moved = primal - primal_step * (unit_rows[None] - adjoint)
        new_primal = jnp.where(free_column, moved, jnp.maximum(moved, 0.0))
        new_capacity = jnp.maximum(capacity - primal_step * (build_cost - capacity_grad), 0.0)
        primal_bar = 2.0 * new_primal - primal
        capacity_bar = 2.0 * new_capacity - capacity
        applied = network_regions(network_forward, primal_bar, net_weights, net_columns)
        earlier = jnp.concatenate([zero_row, primal_bar[:-1, :, 0]], axis=0)
        picked = jnp.einsum('qjr,hrk->hqjk', line_links, primal_bar[:, :, 3], precision=HIGHEST_PRECISION)
        line_flow = jnp.einsum('hqjk,qjkl->hql', picked, line_weights, precision=HIGHEST_PRECISION)
        picked_capacity = jnp.einsum('rgm,rm->rg', selector, capacity_bar, precision=HIGHEST_PRECISION)
        applied = applied.at[:, :, 0].add(-earlier).at[:, :, 1].add(line_flow).at[:, :, 2].add(couple * picked_capacity[None])
        moved_dual = dual + dual_step * (target - applied)
        new_dual = jnp.where(free_row, moved_dual, jnp.maximum(moved_dual, 0.0))
        if iteration + 1 < ITERS:
            primal_total = jnp.sum((new_primal - primal) ** 2) + jnp.sum((new_capacity - capacity) ** 2)
            dual_total = jnp.sum((new_dual - dual) ** 2)
            primal_weight = jnp.sqrt(primal_weight * jnp.sqrt(primal_total / primal_count + EPSILON) / jnp.sqrt(dual_total / dual_count + EPSILON))
        primal, dual, capacity = (new_primal, new_dual, new_capacity)
    return (primal.reshape(hours_all, region_count, row_width), dual.reshape(hours_all, region_count, row_width), capacity)
```

```python
import functools
import math

import jax
import jax.numpy as jnp
from jax import lax
from jax.experimental import pallas as pl
from jax.experimental.pallas import tpu as pltpu
from jax.sharding import PartitionSpec as P

ITERS = 4
STEP_SCALE = 0.2
EPSILON = 1e-06
HIGHEST = lax.Precision.HIGHEST
MESH = pl.DeviceIdType.MESH
F32 = jnp.float32
BF16 = jnp.bfloat16
LOW = float(jnp.finfo(jnp.float32).min)
LANES = 128


def split(value):
    high = value.astype(BF16)
    low = (value - high.astype(F32)).astype(BF16)
    return jnp.concatenate([high, low], axis=0)


def dot_nt(a, b, precision=None):
    return lax.dot_general(
        a, b, (((1,), (1,)), ((), ())), precision=precision, preferred_element_type=F32
    )


def kernel(
    sizes,
    cols_s,
    src_s,
    cap_s,
    build_s,
    gm_v,
    unit_v,
    x_hbm,
    dem_hbm,
    w_hbm,
    lw_hbm,
    x_out,
    y_out,
    cap_out,
    xst,
    dst,
    wst,
    lw,
    wh,
    wl,
    xs,
    ys,
    grad,
    xb,
    yb,
    seg,
    extra,
    table_v,
    table_s,
    rank_v,
    rank_s,
    line_a,
    line_u,
    vx,
    gat0,
    gat,
    pbuf,
    rbuf,
    mt,
    tbuf,
    mr,
    sbuf,
    nb_src,
    nb_dst,
    load_sem,
    w_sem,
    out_sem,
    send_t,
    recv_t,
    send_r,
    recv_r,
    send_g,
    recv_g,
    send_p,
    recv_p,
    send_n,
    recv_n,
):
    (hours, cb, bs, s_count, nl, nt, nr) = sizes
    pairs = cb * s_count
    me_t = lax.axis_index("tm")
    me_r = lax.axis_index("region")
    primal_count = hours * nt * nr * cb * bs + nr * LANES
    dual_count = hours * nt * nr * cb * bs
    couple = 1.0 / math.sqrt(hours * nt)

    cx = pltpu.make_async_copy(x_hbm, xst, load_sem.at[0])
    cd = pltpu.make_async_copy(dem_hbm, dst, load_sem.at[1])
    cl = pltpu.make_async_copy(lw_hbm, lw, load_sem.at[2])
    cx.start()

    barrier = pltpu.get_barrier_semaphore()

    def offset_of(step, count):
        half = (step + 1) // 2
        return count // 2 + jnp.where(step % 2 == 1, half, -half)

    @pl.loop(0, nt - 1)
    def _(step):
        k = offset_of(step, nt)
        pl.semaphore_signal(
            barrier, inc=1, device_id=(lax.rem(me_t + k, nt), me_r), device_id_type=MESH
        )

    @pl.loop(0, nr - 1)
    def _(step):
        k = offset_of(step, nr)
        pl.semaphore_signal(
            barrier, inc=1, device_id=(me_t, lax.rem(me_r + k, nr)), device_id_type=MESH
        )

    cd.start()
    cl.start()
    w_copies = [
        pltpu.make_async_copy(w_hbm.at[i], wst.at[i], w_sem.at[i]) for i in range(cb)
    ]
    for c in w_copies:
        c.start()

    lane = lax.broadcasted_iota(jnp.int32, (1, LANES), 1)
    col_vec = jnp.full((1, LANES), cb, jnp.int32)
    for p in range(pairs):
        col_vec = jnp.where(lane == p, cols_s[p], col_vec)
    rank = jnp.zeros((1, LANES), jnp.int32)
    end_vec = jnp.zeros((1, LANES), jnp.int32)
    for q in range(pairs):
        c = cols_s[q]
        ahead = (col_vec > c) | ((col_vec == c) & (lane > q))
        rank = rank + jnp.where(ahead, 1, 0)
        end_vec = end_vec + jnp.where(lane >= c, 1, 0)
    start_vec = jnp.where(lane == 0, 0, pltpu.roll(end_vec, 1, 1))
    rank_v[...] = rank
    c1 = pltpu.make_async_copy(rank_v, rank_s, load_sem.at[3])
    c1.start()

    own_n = LANES // nt
    cap_vec = jnp.zeros((1, LANES), F32)
    build_vec = jnp.zeros((1, LANES), F32)
    for k in range(own_n):
        here = lane == me_t * own_n + k
        cap_vec = jnp.where(here, cap_s[0, k], cap_vec)
        build_vec = jnp.where(here, build_s[0, k], build_vec)
    mt[0, :, 0:LANES] = cap_vec
    mt[0, :, LANES : 2 * LANES] = build_vec

    cx.wait()
    vx[0:hours, :] = xst[pl.ds(3, hours, stride=cb), :]
    vx[hours : hours + 8, :] = jnp.broadcast_to(unit_v[3], (8, LANES))
    nb_src[0] = xst[pl.ds((hours - 1) * cb, 1), :]

    sel_t = jnp.where(
        gm_v[...] == lax.broadcasted_iota(jnp.int32, (LANES, LANES), 0), 1.0, 0.0
    ).astype(F32)

    pl.semaphore_wait(barrier, nt - 1 + nr - 1)

    def tm_send(r):
        @pl.loop(0, nt - 1)
        def _(step):
            k = offset_of(step, nt)
            pltpu.make_async_remote_copy(
                src_ref=mt.at[r],
                dst_ref=tbuf.at[r, k - 1],
                send_sem=send_t.at[r],
                recv_sem=recv_t.at[r],
                device_id=(lax.rem(me_t + k, nt), me_r),
                device_id_type=MESH,
            ).start()

    def tm_sum(r):
        pltpu.make_async_copy(tbuf.at[r], tbuf.at[r], recv_t.at[r]).wait()
        total = mt[r]
        for k in range(nt - 1):
            total = total + tbuf[r, k]
        return total

    def region_send(src, dst_of, send_sem, recv_sem):
        @pl.loop(0, nr - 1)
        def _(step):
            k = offset_of(step, nr)
            pltpu.make_async_remote_copy(
                src_ref=src(k),
                dst_ref=dst_of(k),
                send_sem=send_sem,
                recv_sem=recv_sem,
                device_id=(me_t, lax.rem(me_r + k, nr)),
                device_id_type=MESH,
            ).start()

    def to_next(n, r, by):
        pltpu.make_async_remote_copy(
            src_ref=nb_src.at[n],
            dst_ref=nb_dst.at[n],
            send_sem=send_n.at[n],
            recv_sem=recv_n.at[n],
            device_id=(lax.rem(me_t + nt + by, nt), me_r),
            device_id_type=MESH,
        ).start()

    def next_wait(n):
        pltpu.make_async_copy(nb_dst.at[n], nb_dst.at[n], recv_n.at[n]).wait()

    region_send(
        lambda k: vx, lambda k: gat0.at[me_r], send_g.at[0], recv_g.at[0]
    )
    tm_send(0)
    to_next(0, 0, 1)
    gat0[me_r] = vx[...]

    def primal_block(c, x, g, step):
        low = jnp.where(c == 3, LOW, 0.0)
        new = jnp.maximum(x - step * g, low)
        change = new - x
        bar = new + change
        xs[c] = new
        xb[c] = split(bar)
        return bar, change * change

    def fold(sq):
        return jnp.sum(sq.reshape(hours // 8, 8, LANES), axis=0)

    c1.wait()
    order = jnp.zeros((1, LANES), jnp.int32)
    order_row = jnp.zeros((1, LANES), jnp.int32)
    order_col = jnp.full((1, LANES), -1, jnp.int32)
    for p in range(pairs):
        here = lane == rank_s[0, p]
        order = jnp.where(here, p, order)
        order_row = jnp.where(here, p // s_count, order_row)
        order_col = jnp.where(here, cols_s[p], order_col)
    goes_on = (order_col == pltpu.roll(order_col, 1, 1)) & (lane > 0)
    table_v[0:1, :] = order
    table_v[1:2, :] = order_row
    table_v[2:3, :] = jnp.where(goes_on, 1, 0)
    table_v[3:4, :] = jnp.maximum(end_vec - 1, 0)
    table_v[4:5, :] = jnp.where(end_vec > start_vec, 1, 0)
    table_v[5:8, :] = jnp.zeros((3, LANES), jnp.int32)
    c2 = pltpu.make_async_copy(table_v, table_s, load_sem.at[4])
    c2.start()

    for i in range(cb):
        w_copies[i].wait()

        @pl.loop(0, s_count)
        def _(s, i=i):
            w = wst[i, s]
            high = w.astype(BF16)
            wh[i * s_count + s] = high
            wl[i * s_count + s] = (w - high.astype(F32)).astype(BF16)

    first_step = STEP_SCALE

    def first_primal(c, acc):
        x = xst[pl.ds(c, hours, stride=cb), :]
        g = jnp.broadcast_to(unit_v[c], (hours, LANES))
        bar, sq = primal_block(c, x, g, first_step)
        return bar, acc + fold(sq)

    zero8 = jnp.zeros((8, LANES), F32)
    bar0, sq_p = first_primal(0, zero8)
    sq_p = lax.fori_loop(1, cb, lambda c, a: first_primal(c, a)[1], sq_p)

    def network(i):
        x3 = jnp.concatenate([xb[cols_s[i * s_count + s]] for s in range(s_count)], axis=1)
        high = jnp.concatenate([wh[i * s_count + s] for s in range(s_count)], axis=0)
        low = jnp.concatenate([wl[i * s_count + s] for s in range(s_count)], axis=0)
        both = jnp.dot(x3, high, preferred_element_type=F32)
        last = jnp.dot(x3[0:hours], low, preferred_element_type=F32)
        return both[0:hours] + both[hours:] + last

    def dual_block(i, target, step, first):
        low = jnp.where(i < 3, LOW, 0.0)
        move = step * (target - network(i))
        if first:
            new = jnp.maximum(move, low)
            change = new
        else:
            old = ys[i]
            new = jnp.maximum(old + move, low)
            change = new - old
        ys[i] = new
        yb[i] = split(new)
        return fold(change * change)

    def target_of(i):
        return dst[pl.ds(i, hours, stride=cb), :]

    def line_apply(block_of):
        parts = jnp.concatenate([block_of(src_s[me_r * nl + j]) for j in range(nl)], axis=1)
        return jnp.dot(parts, lw[...], precision=HIGHEST, preferred_element_type=F32)

    row = lax.broadcasted_iota(jnp.int32, (hours, LANES), 0)
    has_before = jnp.where(me_t > 0, 1.0, 0.0).astype(F32)
    has_after = jnp.where(me_t < nt - 1, 1.0, 0.0).astype(F32)

    def forward(bar0, prev_bar, cap_bar, line_flow, step, first):
        def plain(i, a):
            return a + dual_block(i, target_of(i), step, first)

        sq = lax.fori_loop(3, cb, plain, zero8)
        earlier = pltpu.roll(bar0, 1, 0)
        earlier = jnp.where(row == 0, prev_bar * has_before, earlier)
        extra[0] = target_of(0) + earlier
        picked = jnp.dot(
            jnp.broadcast_to(cap_bar(), (8, LANES)),
            sel_t,
            precision=HIGHEST,
            preferred_element_type=F32,
        )[0:1]
        extra[2] = target_of(2) - couple * picked
        extra[1] = target_of(1) - line_flow()

        def special(i, a):
            return a + dual_block(i, extra[i], step, first)

        return lax.fori_loop(0, 3, special, sq)

    lane_low = lane < LANES // 2

    def pack(p, d):
        p = jnp.sum(p, axis=0, keepdims=True)
        d = jnp.sum(d, axis=0, keepdims=True)
        p = p + pltpu.roll(p, LANES // 2, 1)
        d = d + pltpu.roll(d, LANES // 2, 1)
        return jnp.where(lane_low, p, d)

    cl.wait()
    cd.wait()
    gathered = []

    def first_capacity():
        total = tm_sum(0)
        cap = total[:, 0:LANES]
        build = total[:, LANES : 2 * LANES]
        new_cap = jnp.maximum(cap - first_step * build, 0.0)
        gathered.extend([cap, build, new_cap])
        return new_cap + (new_cap - cap)

    def first_flow():
        pltpu.make_async_copy(
            gat0.at[pl.ds(0, nr - 1)], gat0.at[pl.ds(0, nr - 1)], recv_g.at[0]
        ).wait()
        both = line_apply(lambda q: gat0[q])
        line_unit = both[hours : hours + 1]
        line_x = both[0:hours]
        line_u[...] = jnp.broadcast_to(line_unit, (8, LANES))
        new_line = line_x - first_step * line_unit
        line_a[...] = new_line
        return new_line - first_step * line_unit

    next_wait(0)
    prev_old = nb_dst[0]
    prev_new = jnp.maximum(prev_old - first_step * unit_v[0], 0.0)
    prev_bar = prev_new + (prev_new - prev_old)
    sq_d = forward(bar0, prev_bar, first_capacity, first_flow, first_step, True)
    cap_old, build, cap_new = gathered

    c2.wait()

    def later(it, carry):
        prev_x, cap, cap_change, weight, sq_p, sq_d = carry
        r = it - 1
        mt[it, :, 0:LANES] = jnp.sum(ys[2], axis=0, keepdims=True)
        mt[it, :, LANES : 2 * LANES] = pack(sq_p, sq_d)
        nb_src[1 + r] = ys[0, 0:1, :]
        tm_send(it)
        to_next(1 + r, r, -1)

        terms = dot_nt(ys[1], lw[...].reshape(nl * bs, bs), precision=HIGHEST)
        for k in range(nr):
            q = lax.rem(me_r + k, nr)
            total = jnp.zeros((hours, LANES), F32)
            for j in range(nl):
                on = jnp.where(src_s[me_r * nl + j] == q, 1.0, 0.0).astype(F32)
                total = total + on * terms[:, j * bs : (j + 1) * bs]
            pbuf[r, k] = total
        region_send(
            lambda k: pbuf.at[r, k], lambda k: rbuf.at[r, k - 1], send_p.at[r], recv_p.at[r]
        )

        def pair(n, total):
            p = table_s[0, n]
            y = yb[table_s[1, n]]
            keep = table_s[2, n].astype(F32)
            both = dot_nt(y, wh[p])
            low = dot_nt(y[0:hours], wl[p])
            total = keep * total + (both[0:hours] + both[hours:] + low)
            seg[n] = total
            return total

        lax.fori_loop(0, pairs, pair, jnp.zeros((hours, LANES), F32))

        def gradient(c, _):
            grad[c] = unit_v[c] - table_s[4, c].astype(F32) * seg[table_s[3, c]]
            return 0

        lax.fori_loop(0, cb, gradient, 0)
        nb_src[4 + r] = grad[0, hours - 1 : hours, :]
        to_next(4 + r, r, 1)

        next_wait(1 + r)
        following = pltpu.roll(ys[0], hours - 1, 0)
        following = jnp.where(row == hours - 1, nb_dst[1 + r] * has_after, following)
        grad[0] = grad[0] + following

        total = tm_sum(it)
        col_sums = total[:, 0:LANES]
        region_sums = total[:, LANES : 2 * LANES] + pack(
            cap_change, jnp.zeros_like(cap_change)
        )
        mr[r] = region_sums
        region_send(
            lambda k: mr.at[r], lambda k: sbuf.at[r, k - 1], send_r.at[r], recv_r.at[r]
        )
        capacity_grad = couple * dot_nt(
            jnp.broadcast_to(col_sums, (8, LANES)), sel_t, precision=HIGHEST
        )[0:1]

        pltpu.make_async_copy(rbuf.at[r], rbuf.at[r], recv_p.at[r]).wait()
        line_back = pbuf[r, 0]
        for k in range(nr - 1):
            line_back = line_back + rbuf[r, k]
        flow_grad = grad[3] - line_back
        grad[3] = flow_grad
        gat[r, me_r] = flow_grad
        region_send(
            lambda k: gat.at[r, me_r],
            lambda k: gat.at[r, me_r],
            send_g.at[it],
            recv_g.at[it],
        )
        next_wait(4 + r)
        prev_grad = nb_dst[4 + r] + ys[0, 0:1, :]

        pltpu.make_async_copy(sbuf.at[r], sbuf.at[r], recv_r.at[r]).wait()
        sums = mr[r]
        for k in range(nr - 1):
            sums = sums + sbuf[r, k]
        total_p = jnp.sum(jnp.where(lane_low, sums, 0.0), axis=1, keepdims=True)
        total_d = jnp.sum(jnp.where(lane_low, 0.0, sums), axis=1, keepdims=True)
        total_p = jnp.broadcast_to(total_p, (1, LANES))
        total_d = jnp.broadcast_to(total_d, (1, LANES))
        weight = jnp.sqrt(
            weight
            * jnp.sqrt(total_p / primal_count + EPSILON)
            / jnp.sqrt(total_d / dual_count + EPSILON)
        )
        primal_step = STEP_SCALE / weight
        dual_step = STEP_SCALE * weight

        def primal(c, a):
            bar, sq = primal_block(c, xs[c], grad[c], primal_step)
            return bar, a + fold(sq)

        bar0, sq_p = primal(0, zero8)
        sq_p = lax.fori_loop(1, cb, lambda c, a: primal(c, a)[1], sq_p)
        new_cap = jnp.maximum(cap - primal_step * (build - capacity_grad), 0.0)
        cap_diff = new_cap - cap
        prev_new = jnp.maximum(prev_x - primal_step * prev_grad, 0.0)
        prev_bar = prev_new + (prev_new - prev_x)

        def flow():
            pltpu.make_async_copy(
                gat.at[r, pl.ds(0, nr - 1)], gat.at[r, pl.ds(0, nr - 1)], recv_g.at[it]
            ).wait()
            line_grad = line_apply(lambda q: gat[r, q])
            new_line = line_a[...] - primal_step * line_grad
            line_a[...] = new_line
            return new_line - primal_step * line_grad

        sq_d = forward(bar0, prev_bar, lambda: new_cap + cap_diff, flow, dual_step, False)
        return prev_new, new_cap, cap_diff * cap_diff, weight, sq_p, sq_d

    first_diff = cap_new - cap_old
    carry = (
        prev_new,
        cap_new,
        first_diff * first_diff,
        jnp.ones((1, LANES), F32),
        sq_p,
        sq_d,
    )
    carry = lax.fori_loop(1, ITERS, later, carry)
    cap_out[...] = carry[1]

    def write(c, _):
        xst[pl.ds(c, hours, stride=cb), :] = xs[c]
        dst[pl.ds(c, hours, stride=cb), :] = ys[c]
        return 0

    lax.fori_loop(0, cb, write, 0)
    ox = pltpu.make_async_copy(xst, x_out, out_sem.at[0])
    oy = pltpu.make_async_copy(dst, y_out, out_sem.at[1])
    ox.start()
    oy.start()

    for r in range(ITERS):
        for k in range(nt - 1):
            pltpu.make_async_copy(mt.at[r], mt.at[r], send_t.at[r]).wait()
    pltpu.make_async_copy(
        gat0.at[pl.ds(0, nr - 1)], gat0.at[pl.ds(0, nr - 1)], send_g.at[0]
    ).wait()
    for r in range(ITERS - 1):
        pltpu.make_async_copy(sbuf.at[r], sbuf.at[r], send_r.at[r]).wait()
        pltpu.make_async_copy(rbuf.at[r], rbuf.at[r], send_p.at[r]).wait()
        pltpu.make_async_copy(
            gat.at[r, pl.ds(0, nr - 1)], gat.at[r, pl.ds(0, nr - 1)], send_g.at[r + 1]
        ).wait()
    for n in range(1 + 2 * (ITERS - 1)):
        pltpu.make_async_copy(nb_src.at[n], nb_src.at[n], send_n.at[n]).wait()
    ox.wait()
    oy.wait()


def body(
    start_primal,
    demand,
    unit_cost,
    build_cost,
    start_capacity,
    net_weights,
    net_columns,
    line_weights,
    line_source,
    generator_map,
):
    hours, _, width = start_primal.shape
    bs = net_weights.shape[3]
    cb = width // bs
    s_count = net_weights.shape[2]
    nl = line_weights.shape[1]
    nt = lax.axis_size("tm")
    nr = lax.axis_size("region")
    pairs = cb * s_count
    sizes = (hours, cb, bs, s_count, nl, nt, nr)
    smem = pl.BlockSpec(memory_space=pltpu.SMEM)
    vmem = pl.BlockSpec(memory_space=pltpu.VMEM)
    hbm = pl.BlockSpec(memory_space=pl.ANY)
    rounds = ITERS - 1
    dma = pltpu.SemaphoreType.DMA
    x_new, y_new, cap = pl.pallas_call(
        functools.partial(kernel, sizes),
        out_shape=(
            jax.ShapeDtypeStruct((hours * cb, bs), F32),
            jax.ShapeDtypeStruct((hours * cb, bs), F32),
            jax.ShapeDtypeStruct((1, LANES), F32),
        ),
        in_specs=[smem] * 4 + [vmem] * 2 + [hbm] * 4,
        out_specs=(hbm, hbm, vmem),
        scratch_shapes=[
            pltpu.VMEM((hours * cb, bs), F32),
            pltpu.VMEM((hours * cb, bs), F32),
            pltpu.VMEM((cb, s_count, bs, bs), F32),
            pltpu.VMEM((nl * bs, bs), F32),
            pltpu.VMEM((pairs, bs, bs), BF16),
            pltpu.VMEM((pairs, bs, bs), BF16),
            pltpu.VMEM((cb, hours, bs), F32),
            pltpu.VMEM((cb, hours, bs), F32),
            pltpu.VMEM((cb, hours, bs), F32),
            pltpu.VMEM((cb, 2 * hours, bs), BF16),
            pltpu.VMEM((cb, 2 * hours, bs), BF16),
            pltpu.VMEM((pairs, hours, bs), F32),
            pltpu.VMEM((3, hours, bs), F32),
            pltpu.VMEM((8, LANES), jnp.int32),
            pltpu.SMEM((8, LANES), jnp.int32),
            pltpu.VMEM((1, LANES), jnp.int32),
            pltpu.SMEM((1, LANES), jnp.int32),
            pltpu.VMEM((hours, bs), F32),
            pltpu.VMEM((8, bs), F32),
            pltpu.VMEM((hours + 8, bs), F32),
            pltpu.VMEM((nr, hours + 8, bs), F32),
            pltpu.VMEM((rounds, nr, hours, bs), F32),
            pltpu.VMEM((rounds, nr, hours, bs), F32),
            pltpu.VMEM((rounds, nr - 1, hours, bs), F32),
            pltpu.VMEM((ITERS, 1, 2 * LANES), F32),
            pltpu.VMEM((ITERS, nt - 1, 1, 2 * LANES), F32),
            pltpu.VMEM((rounds, 1, LANES), F32),
            pltpu.VMEM((rounds, nr - 1, 1, LANES), F32),
            pltpu.VMEM((1 + 2 * rounds, 1, LANES), F32),
            pltpu.VMEM((1 + 2 * rounds, 1, LANES), F32),
            dma((5,)),
            dma((cb,)),
            dma((2,)),
            dma((ITERS,)),
            dma((ITERS,)),
            dma((rounds,)),
            dma((rounds,)),
            dma((ITERS,)),
            dma((ITERS,)),
            dma((rounds,)),
            dma((rounds,)),
            dma((1 + 2 * rounds,)),
            dma((1 + 2 * rounds,)),
        ],
        compiler_params=pltpu.CompilerParams(collective_id=0, has_side_effects=True),
    )(
        net_columns.reshape(pairs),
        line_source.reshape(-1),
        start_capacity,
        build_cost,
        generator_map,
        unit_cost.reshape(cb, 1, bs),
        start_primal.reshape(hours * cb, bs),
        demand.reshape(hours * cb, bs),
        net_weights[0],
        line_weights.reshape(nl * bs, bs),
    )
    own = start_capacity.shape[1]
    capacity = lax.dynamic_slice_in_dim(cap, lax.axis_index("tm") * own, own, 1)
    return (
        x_new.reshape(hours, 1, width),
        y_new.reshape(hours, 1, width),
        capacity,
    )


def solution(mesh):
    in_specs = (
        P("tm", "region", None),
        P("tm", "region", None),
        P("region", None),
        P("region", "tm"),
        P("region", "tm"),
        P("region", None, None, None, None),
        P("region", None, None),
        P("region", None, None, None),
        P(),
        P("region", None),
    )
    out_specs = (P("tm", "region", None), P("tm", "region", None), P("region", "tm"))
    return jax.shard_map(body, mesh=mesh, in_specs=in_specs, out_specs=out_specs, check_vma=False)
```

```python
import functools
import math

import jax
import jax.numpy as jnp
from jax import lax
from jax.experimental import pallas as pl
from jax.experimental.pallas import tpu as pltpu
from jax.sharding import PartitionSpec as P

ITERS = 4
STEP_SCALE = 0.2
EPSILON = 1e-06
HIGHEST = lax.Precision.HIGHEST
MESH = pl.DeviceIdType.MESH
F32 = jnp.float32
BF16 = jnp.bfloat16
LOW = float(jnp.finfo(jnp.float32).min)
LANES = 128


def split(value):
    high = value.astype(BF16)
    low = (value - high.astype(F32)).astype(BF16)
    return jnp.concatenate([high, low], axis=0)


def unrolled(first, last, by, step, carry):
    assert (last - first) % by == 0

    def some(n, c):
        for k in range(by):
            c = step(first + n * by + k, c)
        return c

    return lax.fori_loop(0, (last - first) // by, some, carry)


def dot_nt(a, b, precision=None):
    return lax.dot_general(
        a, b, (((1,), (1,)), ((), ())), precision=precision, preferred_element_type=F32
    )


def kernel(
    sizes,
    cols_s,
    src_s,
    cap_s,
    build_s,
    gm_v,
    unit_v,
    x_hbm,
    dem_hbm,
    w_hbm,
    lw_hbm,
    x_out,
    y_out,
    cap_out,
    xst,
    dst,
    wst,
    lw,
    wh,
    wl,
    xs,
    ys,
    grad,
    xb,
    yb,
    seg,
    extra,
    table_v,
    table_s,
    rank_v,
    rank_s,
    line_a,
    line_u,
    vx,
    gat0,
    gat,
    pbuf,
    rbuf,
    mt,
    tbuf,
    mr,
    sbuf,
    nb_src,
    nb_dst,
    load_sem,
    w_sem,
    out_sem,
    send_t,
    recv_t,
    send_r,
    recv_r,
    send_g,
    recv_g,
    send_p,
    recv_p,
    send_n,
    recv_n,
):
    (hours, cb, bs, s_count, nl, nt, nr) = sizes
    pairs = cb * s_count
    me_t = lax.axis_index("tm")
    me_r = lax.axis_index("region")
    primal_count = hours * nt * nr * cb * bs + nr * LANES
    dual_count = hours * nt * nr * cb * bs
    couple = 1.0 / math.sqrt(hours * nt)

    cx = pltpu.make_async_copy(x_hbm, xst, load_sem.at[0])
    cd = pltpu.make_async_copy(dem_hbm, dst, load_sem.at[1])
    cl = pltpu.make_async_copy(lw_hbm, lw, load_sem.at[2])
    cx.start()

    barrier = pltpu.get_barrier_semaphore()

    def offset_of(step, count):
        k = step + count // 2
        return jnp.where(k >= count, k - (count - 1), k)

    def around(me, k, count):
        at = me + k
        return jnp.where(at >= count, at - count, at)

    @pl.loop(0, nt - 1)
    def _(step):
        k = offset_of(step, nt)
        pl.semaphore_signal(
            barrier, inc=1, device_id=(around(me_t, k, nt), me_r), device_id_type=MESH
        )

    @pl.loop(0, nr - 1)
    def _(step):
        k = offset_of(step, nr)
        pl.semaphore_signal(
            barrier, inc=1, device_id=(me_t, around(me_r, k, nr)), device_id_type=MESH
        )

    cd.start()
    cl.start()
    w_copies = [
        pltpu.make_async_copy(w_hbm.at[i], wst.at[i], w_sem.at[i]) for i in range(cb)
    ]
    for c in w_copies:
        c.start()

    lane = lax.broadcasted_iota(jnp.int32, (1, LANES), 1)

    def column(p):
        return cols_s[p % s_count, 0, p // s_count]

    col_vec = jnp.full((1, LANES), cb, jnp.int32)
    for p in range(pairs):
        col_vec = jnp.where(lane == p, column(p), col_vec)
    rank = jnp.zeros((1, LANES), jnp.int32)
    end_vec = jnp.zeros((1, LANES), jnp.int32)
    for q in range(pairs):
        c = column(q)
        ahead = (col_vec > c) | ((col_vec == c) & (lane > q))
        rank = rank + jnp.where(ahead, 1, 0)
        end_vec = end_vec + jnp.where(lane >= c, 1, 0)
    start_vec = jnp.where(lane == 0, 0, pltpu.roll(end_vec, 1, 1))
    rank_v[...] = rank
    c1 = pltpu.make_async_copy(rank_v, rank_s, load_sem.at[3])
    c1.start()

    own_n = LANES // nt
    cap_vec = jnp.zeros((1, LANES), F32)
    build_vec = jnp.zeros((1, LANES), F32)
    for k in range(own_n):
        here = lane == me_t * own_n + k
        cap_vec = jnp.where(here, cap_s[0, k], cap_vec)
        build_vec = jnp.where(here, build_s[0, k], build_vec)
    mt[0, :, 0:LANES] = cap_vec
    mt[0, :, LANES : 2 * LANES] = build_vec

    cx.wait()
    vx[0:hours, :] = xst[pl.ds(3, hours, stride=cb), :]
    vx[hours : hours + 8, :] = jnp.broadcast_to(unit_v[3], (8, LANES))
    nb_src[0] = xst[pl.ds((hours - 1) * cb, 1), :]

    sel_t = jnp.where(
        gm_v[...] == lax.broadcasted_iota(jnp.int32, (LANES, LANES), 0), 1.0, 0.0
    ).astype(F32)

    c1.wait()
    order = jnp.zeros((1, LANES), jnp.int32)
    order_row = jnp.zeros((1, LANES), jnp.int32)
    order_col = jnp.full((1, LANES), -1, jnp.int32)
    for p in range(pairs):
        here = lane == rank_s[0, p]
        order = jnp.where(here, p, order)
        order_row = jnp.where(here, p // s_count, order_row)
        order_col = jnp.where(here, column(p), order_col)
    goes_on = (order_col == pltpu.roll(order_col, 1, 1)) & (lane > 0)
    table_v[0:1, :] = order
    table_v[1:2, :] = order_row
    table_v[2:3, :] = jnp.where(goes_on, 1, 0)
    table_v[3:4, :] = jnp.maximum(end_vec - 1, 0)
    table_v[4:5, :] = jnp.where(end_vec > start_vec, 1, 0)
    table_v[5:8, :] = jnp.zeros((3, LANES), jnp.int32)
    c2 = pltpu.make_async_copy(table_v, table_s, load_sem.at[4])
    c2.start()

    def split_weights(i):
        w_copies[i].wait()

        @pl.loop(0, s_count)
        def _(s):
            w = wst[i, s]
            high = w.astype(BF16)
            wh[i * s_count + s] = high
            wl[i * s_count + s] = (w - high.astype(F32)).astype(BF16)

    for i in range(cb // 2):
        split_weights(i)

    pl.semaphore_wait(barrier, nt - 1 + nr - 1)

    def tm_send(r):
        @pl.loop(0, nt - 1)
        def _(step):
            k = offset_of(step, nt)
            pltpu.make_async_remote_copy(
                src_ref=mt.at[r],
                dst_ref=tbuf.at[r, k - 1],
                send_sem=send_t.at[r],
                recv_sem=recv_t.at[r],
                device_id=(around(me_t, k, nt), me_r),
                device_id_type=MESH,
            ).start()

    def tm_sum(r):
        pltpu.make_async_copy(tbuf.at[r], tbuf.at[r], recv_t.at[r]).wait()
        total = mt[r]
        for k in range(nt - 1):
            total = total + tbuf[r, k]
        return total

    def region_send(src, dst_of, send_sem, recv_sem):
        @pl.loop(0, nr - 1)
        def _(step):
            k = offset_of(step, nr)
            pltpu.make_async_remote_copy(
                src_ref=src(k),
                dst_ref=dst_of(k),
                send_sem=send_sem,
                recv_sem=recv_sem,
                device_id=(me_t, around(me_r, k, nr)),
                device_id_type=MESH,
            ).start()

    def to_next(n, r, by):
        pltpu.make_async_remote_copy(
            src_ref=nb_src.at[n],
            dst_ref=nb_dst.at[n],
            send_sem=send_n.at[n],
            recv_sem=recv_n.at[n],
            device_id=(around(me_t, (by + nt) % nt, nt), me_r),
            device_id_type=MESH,
        ).start()

    def next_wait(n):
        pltpu.make_async_copy(nb_dst.at[n], nb_dst.at[n], recv_n.at[n]).wait()

    region_send(
        lambda k: vx, lambda k: gat0.at[me_r], send_g.at[0], recv_g.at[0]
    )
    tm_send(0)
    to_next(0, 0, 1)
    gat0[me_r] = vx[...]

    def primal_block(c, x, g, step):
        low = jnp.where(c == 3, LOW, 0.0)
        new = jnp.maximum(x - step * g, low)
        change = new - x
        bar = new + change
        xs[c] = new
        xb[c] = split(bar)
        return bar, change * change

    def fold(sq):
        return jnp.sum(sq.reshape(hours // 8, 8, LANES), axis=0)

    for i in range(cb // 2, cb):
        split_weights(i)

    first_step = STEP_SCALE

    def first_primal(c, acc):
        x = xst[pl.ds(c, hours, stride=cb), :]
        g = jnp.broadcast_to(unit_v[c], (hours, LANES))
        bar, sq = primal_block(c, x, g, first_step)
        return bar, acc + fold(sq)

    zero8 = jnp.zeros((8, LANES), F32)
    bar0, sq_p = first_primal(0, zero8)
    sq_p = unrolled(1, cb, 4, lambda c, a: first_primal(c, a)[1], sq_p)

    def network(i):
        x3 = jnp.concatenate([xb[cols_s[s, 0, i]] for s in range(s_count)], axis=1)
        high = jnp.concatenate([wh[i * s_count + s] for s in range(s_count)], axis=0)
        low = jnp.concatenate([wl[i * s_count + s] for s in range(s_count)], axis=0)
        both = jnp.dot(x3, high, preferred_element_type=F32)
        last = jnp.dot(x3[0:hours], low, preferred_element_type=F32)
        return both[0:hours] + both[hours:] + last

    def dual_block(i, target, step, first):
        low = jnp.where(i < 3, LOW, 0.0)
        move = step * (target - network(i))
        if first:
            new = jnp.maximum(move, low)
            change = new
        else:
            old = ys[i]
            new = jnp.maximum(old + move, low)
            change = new - old
        ys[i] = new
        yb[i] = split(new)
        return fold(change * change)

    def target_of(i):
        return dst[pl.ds(i, hours, stride=cb), :]

    def line_apply(block_of):
        parts = jnp.concatenate([block_of(src_s[j, me_r]) for j in range(nl)], axis=1)
        return jnp.dot(parts, lw[...], precision=HIGHEST, preferred_element_type=F32)

    row = lax.broadcasted_iota(jnp.int32, (hours, LANES), 0)
    has_before = jnp.where(me_t > 0, 1.0, 0.0).astype(F32)
    has_after = jnp.where(me_t < nt - 1, 1.0, 0.0).astype(F32)

    def forward(bar0, prev_bar, cap_bar, line_flow, step, first):
        def plain(i, a):
            return a + dual_block(i, target_of(i), step, first)

        sq = unrolled(3, cb, 11, plain, zero8)
        earlier = pltpu.roll(bar0, 1, 0)
        earlier = jnp.where(row == 0, prev_bar * has_before, earlier)
        extra[0] = target_of(0) + earlier
        picked = jnp.dot(
            jnp.broadcast_to(cap_bar(), (8, LANES)),
            sel_t,
            precision=HIGHEST,
            preferred_element_type=F32,
        )[0:1]
        extra[2] = target_of(2) - couple * picked
        sq = sq + dual_block(0, extra[0], step, first)
        sq = sq + dual_block(2, extra[2], step, first)
        extra[1] = target_of(1) - line_flow()
        return sq + dual_block(1, extra[1], step, first)

    lane_low = lane < LANES // 2

    def pack(p, d):
        p = jnp.sum(p, axis=0, keepdims=True)
        d = jnp.sum(d, axis=0, keepdims=True)
        p = p + pltpu.roll(p, LANES // 2, 1)
        d = d + pltpu.roll(d, LANES // 2, 1)
        return jnp.where(lane_low, p, d)

    cl.wait()
    cd.wait()
    gathered = []

    def first_capacity():
        total = tm_sum(0)
        cap = total[:, 0:LANES]
        build = total[:, LANES : 2 * LANES]
        new_cap = jnp.maximum(cap - first_step * build, 0.0)
        gathered.extend([cap, build, new_cap])
        return new_cap + (new_cap - cap)

    def first_flow():
        pltpu.make_async_copy(
            gat0.at[pl.ds(0, nr - 1)], gat0.at[pl.ds(0, nr - 1)], recv_g.at[0]
        ).wait()
        both = line_apply(lambda q: gat0[q])
        line_unit = both[hours : hours + 1]
        line_x = both[0:hours]
        line_u[...] = jnp.broadcast_to(line_unit, (8, LANES))
        new_line = line_x - first_step * line_unit
        line_a[...] = new_line
        return new_line - first_step * line_unit

    next_wait(0)
    prev_old = nb_dst[0]
    prev_new = jnp.maximum(prev_old - first_step * unit_v[0], 0.0)
    prev_bar = prev_new + (prev_new - prev_old)
    sq_d = forward(bar0, prev_bar, first_capacity, first_flow, first_step, True)
    cap_old, build, cap_new = gathered

    c2.wait()

    def later(it, carry):
        prev_x, cap, cap_change, weight, sq_p, sq_d = carry
        r = it - 1
        mt[it, :, 0:LANES] = jnp.sum(ys[2], axis=0, keepdims=True)
        mt[it, :, LANES : 2 * LANES] = pack(sq_p, sq_d)
        nb_src[1 + r] = ys[0, 0:1, :]
        tm_send(it)
        to_next(1 + r, r, -1)

        terms = dot_nt(ys[1], lw[...].reshape(nl * bs, bs), precision=HIGHEST)
        for k in range(nr):
            q = around(me_r, k, nr)
            total = jnp.zeros((hours, LANES), F32)
            for j in range(nl):
                on = jnp.where(src_s[j, me_r] == q, 1.0, 0.0).astype(F32)
                total = total + on * terms[:, j * bs : (j + 1) * bs]
            pbuf[r, k] = total
        region_send(
            lambda k: pbuf.at[r, k], lambda k: rbuf.at[r, k - 1], send_p.at[r], recv_p.at[r]
        )

        def pair(n, total):
            p = table_s[0, n]
            y = yb[table_s[1, n]]
            keep = table_s[2, n].astype(F32)
            both = dot_nt(y, wh[p])
            low = dot_nt(y[0:hours], wl[p])
            total = keep * total + (both[0:hours] + both[hours:] + low)
            seg[n] = total
            return total

        unrolled(0, pairs, 15, pair, jnp.zeros((hours, LANES), F32))

        def gradient(c, _):
            grad[c] = unit_v[c] - table_s[4, c].astype(F32) * seg[table_s[3, c]]
            return 0

        unrolled(0, cb, 5, gradient, 0)
        nb_src[4 + r] = grad[0, hours - 1 : hours, :]
        to_next(4 + r, r, 1)

        next_wait(1 + r)
        following = pltpu.roll(ys[0], hours - 1, 0)
        following = jnp.where(row == hours - 1, nb_dst[1 + r] * has_after, following)
        grad[0] = grad[0] + following

        total = tm_sum(it)
        col_sums = total[:, 0:LANES]
        region_sums = total[:, LANES : 2 * LANES] + pack(
            cap_change, jnp.zeros_like(cap_change)
        )
        mr[r] = region_sums
        region_send(
            lambda k: mr.at[r], lambda k: sbuf.at[r, k - 1], send_r.at[r], recv_r.at[r]
        )
        capacity_grad = couple * dot_nt(
            jnp.broadcast_to(col_sums, (8, LANES)), sel_t, precision=HIGHEST
        )[0:1]

        pltpu.make_async_copy(rbuf.at[r], rbuf.at[r], recv_p.at[r]).wait()
        line_back = pbuf[r, 0]
        for k in range(nr - 1):
            line_back = line_back + rbuf[r, k]
        flow_grad = grad[3] - line_back
        grad[3] = flow_grad
        gat[r, me_r] = flow_grad
        region_send(
            lambda k: gat.at[r, me_r],
            lambda k: gat.at[r, me_r],
            send_g.at[it],
            recv_g.at[it],
        )
        next_wait(4 + r)
        prev_grad = nb_dst[4 + r] + ys[0, 0:1, :]

        pltpu.make_async_copy(sbuf.at[r], sbuf.at[r], recv_r.at[r]).wait()
        sums = mr[r]
        for k in range(nr - 1):
            sums = sums + sbuf[r, k]
        total_p = jnp.sum(jnp.where(lane_low, sums, 0.0), axis=1, keepdims=True)
        total_d = jnp.sum(jnp.where(lane_low, 0.0, sums), axis=1, keepdims=True)
        total_p = jnp.broadcast_to(total_p, (1, LANES))
        total_d = jnp.broadcast_to(total_d, (1, LANES))
        weight = jnp.sqrt(
            weight
            * jnp.sqrt(total_p / primal_count + EPSILON)
            / jnp.sqrt(total_d / dual_count + EPSILON)
        )
        primal_step = STEP_SCALE / weight
        dual_step = STEP_SCALE * weight

        def primal(c, a):
            bar, sq = primal_block(c, xs[c], grad[c], primal_step)
            return bar, a + fold(sq)

        bar0, sq_p = primal(0, zero8)
        sq_p = unrolled(1, cb, 6, lambda c, a: primal(c, a)[1], sq_p)
        new_cap = jnp.maximum(cap - primal_step * (build - capacity_grad), 0.0)
        cap_diff = new_cap - cap
        prev_new = jnp.maximum(prev_x - primal_step * prev_grad, 0.0)
        prev_bar = prev_new + (prev_new - prev_x)

        def flow():
            pltpu.make_async_copy(
                gat.at[r, pl.ds(0, nr - 1)], gat.at[r, pl.ds(0, nr - 1)], recv_g.at[it]
            ).wait()
            line_grad = line_apply(lambda q: gat[r, q])
            new_line = line_a[...] - primal_step * line_grad
            line_a[...] = new_line
            return new_line - primal_step * line_grad

        sq_d = forward(bar0, prev_bar, lambda: new_cap + cap_diff, flow, dual_step, False)
        return prev_new, new_cap, cap_diff * cap_diff, weight, sq_p, sq_d

    first_diff = cap_new - cap_old
    carry = (
        prev_new,
        cap_new,
        first_diff * first_diff,
        jnp.ones((1, LANES), F32),
        sq_p,
        sq_d,
    )
    carry = lax.fori_loop(1, ITERS, later, carry)
    cap_out[...] = carry[1]

    ox = pltpu.make_async_copy(xs, x_out, out_sem.at[0])
    oy = pltpu.make_async_copy(ys, y_out, out_sem.at[1])
    ox.start()
    oy.start()

    for r in range(ITERS):
        pltpu.make_async_copy(tbuf.at[r], tbuf.at[r], send_t.at[r]).wait()
    pltpu.make_async_copy(
        gat0.at[pl.ds(0, nr - 1)], gat0.at[pl.ds(0, nr - 1)], send_g.at[0]
    ).wait()
    for r in range(ITERS - 1):
        pltpu.make_async_copy(sbuf.at[r], sbuf.at[r], send_r.at[r]).wait()
        pltpu.make_async_copy(rbuf.at[r], rbuf.at[r], send_p.at[r]).wait()
        pltpu.make_async_copy(
            gat.at[r, pl.ds(0, nr - 1)], gat.at[r, pl.ds(0, nr - 1)], send_g.at[r + 1]
        ).wait()
    for n in range(1 + 2 * (ITERS - 1)):
        pltpu.make_async_copy(nb_src.at[n], nb_src.at[n], send_n.at[n]).wait()
    ox.wait()
    oy.wait()


def by_hour(x, y):
    cb, hours, bs = x.shape
    some = min(16, hours)

    def place(x_ref, y_ref, x_out, y_out):
        for c in range(cb):
            x_out[pl.ds(c, some, stride=cb), :] = x_ref[c]
            y_out[pl.ds(c, some, stride=cb), :] = y_ref[c]

    block = pl.BlockSpec((cb, some, bs), lambda i: (0, i, 0))
    out = pl.BlockSpec((some * cb, bs), lambda i: (i, 0))
    shape = jax.ShapeDtypeStruct((hours * cb, bs), F32)
    return pl.pallas_call(
        place,
        grid=(hours // some,),
        in_specs=[block, block],
        out_specs=(out, out),
        out_shape=(shape, shape),
    )(x, y)


def body(
    start_primal,
    demand,
    unit_cost,
    build_cost,
    start_capacity,
    net_weights,
    net_columns,
    line_weights,
    line_source,
    generator_map,
):
    hours, _, width = start_primal.shape
    bs = net_weights.shape[3]
    cb = width // bs
    s_count = net_weights.shape[2]
    nl = line_weights.shape[1]
    nt = lax.axis_size("tm")
    nr = lax.axis_size("region")
    pairs = cb * s_count
    sizes = (hours, cb, bs, s_count, nl, nt, nr)
    smem = pl.BlockSpec(memory_space=pltpu.SMEM)
    vmem = pl.BlockSpec(memory_space=pltpu.VMEM)
    hbm = pl.BlockSpec(memory_space=pl.ANY)
    rounds = ITERS - 1
    dma = pltpu.SemaphoreType.DMA
    x_new, y_new, cap = pl.pallas_call(
        functools.partial(kernel, sizes),
        out_shape=(
            jax.ShapeDtypeStruct((cb, hours, bs), F32),
            jax.ShapeDtypeStruct((cb, hours, bs), F32),
            jax.ShapeDtypeStruct((1, LANES), F32),
        ),
        in_specs=[smem] * 4 + [vmem] * 2 + [hbm] * 4,
        out_specs=(hbm, hbm, vmem),
        scratch_shapes=[
            pltpu.VMEM((hours * cb, bs), F32),
            pltpu.VMEM((hours * cb, bs), F32),
            pltpu.VMEM((cb, s_count, bs, bs), F32),
            pltpu.VMEM((nl * bs, bs), F32),
            pltpu.VMEM((pairs, bs, bs), BF16),
            pltpu.VMEM((pairs, bs, bs), BF16),
            pltpu.VMEM((cb, hours, bs), F32),
            pltpu.VMEM((cb, hours, bs), F32),
            pltpu.VMEM((cb, hours, bs), F32),
            pltpu.VMEM((cb, 2 * hours, bs), BF16),
            pltpu.VMEM((cb, 2 * hours, bs), BF16),
            pltpu.VMEM((pairs, hours, bs), F32),
            pltpu.VMEM((3, hours, bs), F32),
            pltpu.VMEM((8, LANES), jnp.int32),
            pltpu.SMEM((8, LANES), jnp.int32),
            pltpu.VMEM((1, LANES), jnp.int32),
            pltpu.SMEM((1, LANES), jnp.int32),
            pltpu.VMEM((hours, bs), F32),
            pltpu.VMEM((8, bs), F32),
            pltpu.VMEM((hours + 8, bs), F32),
            pltpu.VMEM((nr, hours + 8, bs), F32),
            pltpu.VMEM((rounds, nr, hours, bs), F32),
            pltpu.VMEM((rounds, nr, hours, bs), F32),
            pltpu.VMEM((rounds, nr - 1, hours, bs), F32),
            pltpu.VMEM((ITERS, 1, 2 * LANES), F32),
            pltpu.VMEM((ITERS, nt - 1, 1, 2 * LANES), F32),
            pltpu.VMEM((rounds, 1, LANES), F32),
            pltpu.VMEM((rounds, nr - 1, 1, LANES), F32),
            pltpu.VMEM((1 + 2 * rounds, 1, LANES), F32),
            pltpu.VMEM((1 + 2 * rounds, 1, LANES), F32),
            dma((5,)),
            dma((cb,)),
            dma((2,)),
            dma((ITERS,)),
            dma((ITERS,)),
            dma((rounds,)),
            dma((rounds,)),
            dma((ITERS,)),
            dma((ITERS,)),
            dma((rounds,)),
            dma((rounds,)),
            dma((1 + 2 * rounds,)),
            dma((1 + 2 * rounds,)),
        ],
        compiler_params=pltpu.CompilerParams(collective_id=0, has_side_effects=True),
    )(
        jnp.transpose(net_columns, (2, 0, 1)),
        jnp.transpose(line_source),
        start_capacity,
        build_cost,
        generator_map,
        unit_cost.reshape(cb, 1, bs),
        start_primal.reshape(hours * cb, bs),
        demand.reshape(hours * cb, bs),
        net_weights[0],
        line_weights.reshape(nl * bs, bs),
    )
    own = start_capacity.shape[1]
    x_new, y_new = by_hour(x_new, y_new)
    capacity = lax.dynamic_slice_in_dim(cap, lax.axis_index("tm") * own, own, 1)
    return (
        x_new.reshape(hours, 1, width),
        y_new.reshape(hours, 1, width),
        capacity,
    )


def solution(mesh):
    in_specs = (
        P("tm", "region", None),
        P("tm", "region", None),
        P("region", None),
        P("region", "tm"),
        P("region", "tm"),
        P("region", None, None, None, None),
        P("region", None, None),
        P("region", None, None, None),
        P(),
        P("region", None),
    )
    out_specs = (P("tm", "region", None), P("tm", "region", None), P("region", "tm"))
    return jax.shard_map(body, mesh=mesh, in_specs=in_specs, out_specs=out_specs, check_vma=False)
```

```python
import functools
import math

import jax
import jax.numpy as jnp
from jax import lax
from jax.experimental import pallas as pl
from jax.experimental.pallas import tpu as pltpu
from jax.sharding import PartitionSpec as P

ITERS = 4
STEP_SCALE = 0.2
EPSILON = 1e-06
HIGHEST = lax.Precision.HIGHEST
MESH = pl.DeviceIdType.MESH
F32 = jnp.float32
BF16 = jnp.bfloat16
LOW = float(jnp.finfo(jnp.float32).min)
LANES = 128


def split(value):
    high = value.astype(BF16)
    low = (value - high.astype(F32)).astype(BF16)
    return jnp.concatenate([high, low], axis=0)


def unrolled(first, last, by, step, carry):
    assert (last - first) % by == 0

    def some(n, c):
        for k in range(by):
            c = step(first + n * by + k, c)
        return c

    return lax.fori_loop(0, (last - first) // by, some, carry)


def dot_nt(a, b, precision=None):
    return lax.dot_general(
        a, b, (((1,), (1,)), ((), ())), precision=precision, preferred_element_type=F32
    )


def kernel(
    sizes,
    cols_s,
    src_s,
    cap_s,
    build_s,
    gm_v,
    unit_v,
    x_hbm,
    dem_hbm,
    w_hbm,
    lw_hbm,
    xs,
    ys,
    cap_out,
    xst,
    dst,
    wst,
    lw,
    lwh,
    lwl,
    wh,
    wl,
    tgt,
    grad,
    xb,
    yb,
    seg,
    extra,
    table_v,
    table_s,
    rank_v,
    rank_s,
    line_a,
    line_u,
    vx,
    gat0,
    gat,
    pbuf,
    rbuf,
    mt,
    tbuf,
    mr,
    sbuf,
    nb_src,
    nb_dst,
    load_sem,
    w_sem,
    send_t,
    recv_t,
    send_r,
    recv_r,
    send_g,
    recv_g,
    send_p,
    recv_p,
    send_n,
    recv_n,
):
    (hours, cb, bs, s_count, nl, nt, nr) = sizes
    pairs = cb * s_count
    me_t = lax.axis_index("tm")
    me_r = lax.axis_index("region")
    primal_count = hours * nt * nr * cb * bs + nr * LANES
    dual_count = hours * nt * nr * cb * bs
    couple = 1.0 / math.sqrt(hours * nt)

    cx = pltpu.make_async_copy(x_hbm, xst, load_sem.at[0])
    cd = pltpu.make_async_copy(dem_hbm, dst, load_sem.at[1])
    cl = pltpu.make_async_copy(lw_hbm, lw, load_sem.at[2])
    cx.start()

    barrier = pltpu.get_barrier_semaphore()

    def offset_of(step, count):
        k = step + count // 2
        return jnp.where(k >= count, k - (count - 1), k)

    def around(me, k, count):
        at = me + k
        return jnp.where(at >= count, at - count, at)

    nx = 4 if nt % 4 == 0 else 1
    nz = nt // nx
    me_z, me_x = me_t // nx, me_t % nx

    def tm_partners(act):
        order = [(dz, dx) for dz in range(nz) for dx in range(nx) if dz or dx]
        order.sort(key=lambda d: -min(d[0], nz - d[0]) - min(d[1], nx - d[1]))
        for dz, dx in order:
            act(dz * nx + dx - 1, around(me_z, dz, nz) * nx + around(me_x, dx, nx))

    tm_partners(
        lambda slot, at: pl.semaphore_signal(
            barrier, inc=1, device_id=(at, me_r), device_id_type=MESH
        )
    )

    @pl.loop(0, nr - 1)
    def _(step):
        k = offset_of(step, nr)
        pl.semaphore_signal(
            barrier, inc=1, device_id=(me_t, around(me_r, k, nr)), device_id_type=MESH
        )

    cd.start()
    cl.start()
    w_copies = [
        pltpu.make_async_copy(w_hbm.at[i], wst.at[i], w_sem.at[i]) for i in range(cb)
    ]
    for c in w_copies:
        c.start()

    lane = lax.broadcasted_iota(jnp.int32, (1, LANES), 1)

    def column(p):
        return cols_s[p % s_count, 0, p // s_count]

    col_vec = jnp.full((1, LANES), cb, jnp.int32)
    for p in range(pairs):
        col_vec = jnp.where(lane == p, column(p), col_vec)
    rank = jnp.zeros((1, LANES), jnp.int32)
    end_vec = jnp.zeros((1, LANES), jnp.int32)
    for q in range(pairs):
        c = column(q)
        ahead = (col_vec > c) | ((col_vec == c) & (lane > q))
        rank = rank + jnp.where(ahead, 1, 0)
        end_vec = end_vec + jnp.where(lane >= c, 1, 0)
    start_vec = jnp.where(lane == 0, 0, pltpu.roll(end_vec, 1, 1))
    rank_v[...] = rank
    c1 = pltpu.make_async_copy(rank_v, rank_s, load_sem.at[3])
    c1.start()

    own_n = LANES // nt
    cap_vec = jnp.zeros((1, LANES), F32)
    build_vec = jnp.zeros((1, LANES), F32)
    for k in range(own_n):
        here = lane == me_t * own_n + k
        cap_vec = jnp.where(here, cap_s[0, k], cap_vec)
        build_vec = jnp.where(here, build_s[0, k], build_vec)
    mt[0, :, 0:LANES] = cap_vec
    mt[0, :, LANES : 2 * LANES] = build_vec

    cx.wait()
    vx[0:hours, :] = xst[pl.ds(3, hours, stride=cb), :]
    vx[hours : hours + 8, :] = jnp.broadcast_to(unit_v[3], (8, LANES))
    nb_src[0] = xst[pl.ds((hours - 1) * cb, 1), :]

    sel_t = jnp.where(
        gm_v[...] == lax.broadcasted_iota(jnp.int32, (LANES, LANES), 0), 1.0, 0.0
    ).astype(F32)

    c1.wait()
    order = jnp.zeros((1, LANES), jnp.int32)
    order_row = jnp.zeros((1, LANES), jnp.int32)
    order_col = jnp.full((1, LANES), -1, jnp.int32)
    for p in range(pairs):
        here = lane == rank_s[0, p]
        order = jnp.where(here, p, order)
        order_row = jnp.where(here, p // s_count, order_row)
        order_col = jnp.where(here, column(p), order_col)
    goes_on = (order_col == pltpu.roll(order_col, 1, 1)) & (lane > 0)
    table_v[0:1, :] = order
    table_v[1:2, :] = order_row
    table_v[2:3, :] = jnp.where(goes_on, 1, 0)
    table_v[3:4, :] = jnp.maximum(end_vec - 1, 0)
    table_v[4:5, :] = jnp.where(end_vec > start_vec, 1, 0)
    table_v[5:8, :] = jnp.zeros((3, LANES), jnp.int32)
    c2 = pltpu.make_async_copy(table_v, table_s, load_sem.at[4])
    c2.start()

    def split_weights(i):
        w_copies[i].wait()

        @pl.loop(0, s_count)
        def _(s):
            w = wst[i, s]
            high = w.astype(BF16)
            wh[i * s_count + s] = high
            wl[i * s_count + s] = (w - high.astype(F32)).astype(BF16)

    for i in range(cb // 2):
        split_weights(i)

    cd.wait()
    cl.wait()

    def place_target(i, _):
        tgt[i] = dst[pl.ds(i, hours, stride=cb), :]
        return 0

    unrolled(0, cb, 5, place_target, 0)
    line_high = lw[...].astype(BF16)
    lwh[...] = line_high
    lwl[...] = (lw[...] - line_high.astype(F32)).astype(BF16)

    pl.semaphore_wait(barrier, nt - 1 + nr - 1)

    def tm_send(r):
        def send(slot, at):
            pltpu.make_async_remote_copy(
                src_ref=mt.at[r],
                dst_ref=tbuf.at[r, slot],
                send_sem=send_t.at[r],
                recv_sem=recv_t.at[r],
                device_id=(at, me_r),
                device_id_type=MESH,
            ).start()

        tm_partners(send)

    def tm_sum(r):
        pltpu.make_async_copy(tbuf.at[r], tbuf.at[r], recv_t.at[r]).wait()
        total = mt[r]
        for k in range(nt - 1):
            total = total + tbuf[r, k]
        return total

    def region_send(src, dst_of, send_sem, recv_sem):
        @pl.loop(0, nr - 1)
        def _(step):
            k = offset_of(step, nr)
            pltpu.make_async_remote_copy(
                src_ref=src(k),
                dst_ref=dst_of(k),
                send_sem=send_sem,
                recv_sem=recv_sem,
                device_id=(me_t, around(me_r, k, nr)),
                device_id_type=MESH,
            ).start()

    def to_next(n, r, by):
        pltpu.make_async_remote_copy(
            src_ref=nb_src.at[n],
            dst_ref=nb_dst.at[n],
            send_sem=send_n.at[n],
            recv_sem=recv_n.at[n],
            device_id=(around(me_t, (by + nt) % nt, nt), me_r),
            device_id_type=MESH,
        ).start()

    def next_wait(n):
        pltpu.make_async_copy(nb_dst.at[n], nb_dst.at[n], recv_n.at[n]).wait()

    region_send(
        lambda k: vx, lambda k: gat0.at[me_r], send_g.at[0], recv_g.at[0]
    )
    tm_send(0)
    to_next(0, 0, 1)
    gat0[me_r] = vx[...]

    def primal_block(c, x, g, step):
        low = jnp.where(c == 3, LOW, 0.0)
        new = jnp.maximum(x - step * g, low)
        change = new - x
        bar = new + change
        xs[c] = new
        xb[c] = split(bar)
        return bar, change * change

    def fold(sq):
        return jnp.sum(sq.reshape(hours // 8, 8, LANES), axis=0)

    for i in range(cb // 2, cb):
        split_weights(i)

    first_step = STEP_SCALE

    def first_primal(c, acc):
        x = xst[pl.ds(c, hours, stride=cb), :]
        g = jnp.broadcast_to(unit_v[c], (hours, LANES))
        bar, sq = primal_block(c, x, g, first_step)
        return bar, acc + fold(sq)

    zero8 = jnp.zeros((8, LANES), F32)
    bar0, sq_p = first_primal(0, zero8)
    sq_p = unrolled(1, cb, 4, lambda c, a: first_primal(c, a)[1], sq_p)

    def network(i):
        x3 = jnp.concatenate([xb[cols_s[s, 0, i]] for s in range(s_count)], axis=1)
        high = jnp.concatenate([wh[i * s_count + s] for s in range(s_count)], axis=0)
        low = jnp.concatenate([wl[i * s_count + s] for s in range(s_count)], axis=0)
        both = jnp.dot(x3, high, preferred_element_type=F32)
        last = jnp.dot(x3[0:hours], low, preferred_element_type=F32)
        return both[0:hours] + both[hours:] + last

    def dual_block(i, rest, step, first):
        low = jnp.where(i < 3, LOW, 0.0)
        move = step * rest
        if first:
            new = jnp.maximum(move, low)
            change = new
        else:
            old = ys[i]
            new = jnp.maximum(old + move, low)
            change = new - old
        ys[i] = new
        yb[i] = split(new)
        return fold(change * change)

    def target_of(i):
        return dst[pl.ds(i, hours, stride=cb), :]

    def line_apply(block_of):
        parts = jnp.concatenate([block_of(src_s[j, me_r]) for j in range(nl)], axis=1)
        high = parts.astype(BF16)
        low = (parts - high.astype(F32)).astype(BF16)
        return (
            jnp.dot(high, lwh[...], preferred_element_type=F32)
            + jnp.dot(low, lwh[...], preferred_element_type=F32)
            + jnp.dot(high, lwl[...], preferred_element_type=F32)
        )

    row = lax.broadcasted_iota(jnp.int32, (hours, LANES), 0)
    has_before = jnp.where(me_t > 0, 1.0, 0.0).astype(F32)
    has_after = jnp.where(me_t < nt - 1, 1.0, 0.0).astype(F32)

    def forward(bar0, prev_bar, cap_bar, line_flow, step, first):
        earlier = pltpu.roll(bar0, 1, 0)
        earlier = jnp.where(row == 0, prev_bar * has_before, earlier)
        tgt[0] = target_of(0) + earlier
        picked = jnp.dot(
            jnp.broadcast_to(cap_bar(), (8, LANES)),
            sel_t,
            precision=HIGHEST,
            preferred_element_type=F32,
        )[0:1]
        tgt[2] = target_of(2) - couple * picked
        tgt[1] = target_of(1) - network(1)

        def plain(n, a):
            i = jnp.where(n > 0, n + 1, 0)
            return a + dual_block(i, tgt[i] - network(i), step, first)

        sq = unrolled(0, cb - 1, 12, plain, zero8)
        return sq + dual_block(1, tgt[1] - line_flow(), step, first)

    lane_low = lane < LANES // 2

    def pack(p, d):
        p = jnp.sum(p, axis=0, keepdims=True)
        d = jnp.sum(d, axis=0, keepdims=True)
        p = p + pltpu.roll(p, LANES // 2, 1)
        d = d + pltpu.roll(d, LANES // 2, 1)
        return jnp.where(lane_low, p, d)

    gathered = []

    def first_capacity():
        total = tm_sum(0)
        cap = total[:, 0:LANES]
        build = total[:, LANES : 2 * LANES]
        new_cap = jnp.maximum(cap - first_step * build, 0.0)
        gathered.extend([cap, build, new_cap])
        return new_cap + (new_cap - cap)

    def first_flow():
        pltpu.make_async_copy(
            gat0.at[pl.ds(0, nr - 1)], gat0.at[pl.ds(0, nr - 1)], recv_g.at[0]
        ).wait()
        both = line_apply(lambda q: gat0[q])
        line_unit = both[hours : hours + 1]
        line_x = both[0:hours]
        line_u[...] = jnp.broadcast_to(line_unit, (8, LANES))
        new_line = line_x - first_step * line_unit
        line_a[...] = new_line
        return new_line - first_step * line_unit

    next_wait(0)
    prev_old = nb_dst[0]
    prev_new = jnp.maximum(prev_old - first_step * unit_v[0], 0.0)
    prev_bar = prev_new + (prev_new - prev_old)
    sq_d = forward(bar0, prev_bar, first_capacity, first_flow, first_step, True)
    cap_old, build, cap_new = gathered

    c2.wait()

    def later(it, carry):
        prev_x, cap, cap_change, weight, sq_p, sq_d = carry
        r = it - 1
        mt[it, :, 0:LANES] = jnp.sum(ys[2], axis=0, keepdims=True)
        mt[it, :, LANES : 2 * LANES] = pack(sq_p, sq_d)
        nb_src[1 + r] = ys[0, 0:1, :]
        tm_send(it)
        to_next(1 + r, r, -1)

        y1 = yb[1]
        terms = (
            dot_nt(y1[0:hours], lwh[...])
            + dot_nt(y1[hours:], lwh[...])
            + dot_nt(y1[0:hours], lwl[...])
        )
        for k in range(nr):
            q = around(me_r, k, nr)
            total = jnp.zeros((hours, LANES), F32)
            for j in range(nl):
                on = jnp.where(src_s[j, me_r] == q, 1.0, 0.0).astype(F32)
                total = total + on * terms[:, j * bs : (j + 1) * bs]
            pbuf[r, k] = total
        region_send(
            lambda k: pbuf.at[r, k], lambda k: rbuf.at[r, k - 1], send_p.at[r], recv_p.at[r]
        )

        def pair(n, total):
            p = table_s[0, n]
            y = yb[table_s[1, n]]
            keep = table_s[2, n].astype(F32)
            both = dot_nt(y, wh[p])
            low = dot_nt(y[0:hours], wl[p])
            total = keep * total + (both[0:hours] + both[hours:] + low)
            seg[n] = total
            return total

        unrolled(0, pairs, 15, pair, jnp.zeros((hours, LANES), F32))

        def gradient(c, _):
            grad[c] = unit_v[c] - table_s[4, c].astype(F32) * seg[table_s[3, c]]
            return 0

        unrolled(0, cb, 5, gradient, 0)
        nb_src[4 + r] = grad[0, hours - 1 : hours, :]
        to_next(4 + r, r, 1)

        next_wait(1 + r)
        following = pltpu.roll(ys[0], hours - 1, 0)
        following = jnp.where(row == hours - 1, nb_dst[1 + r] * has_after, following)
        grad[0] = grad[0] + following

        total = tm_sum(it)
        col_sums = total[:, 0:LANES]
        region_sums = total[:, LANES : 2 * LANES] + pack(
            cap_change, jnp.zeros_like(cap_change)
        )
        mr[r] = region_sums
        region_send(
            lambda k: mr.at[r], lambda k: sbuf.at[r, k - 1], send_r.at[r], recv_r.at[r]
        )
        capacity_grad = couple * dot_nt(
            jnp.broadcast_to(col_sums, (8, LANES)), sel_t, precision=HIGHEST
        )[0:1]

        pltpu.make_async_copy(rbuf.at[r], rbuf.at[r], recv_p.at[r]).wait()
        line_back = pbuf[r, 0]
        for k in range(nr - 1):
            line_back = line_back + rbuf[r, k]
        flow_grad = grad[3] - line_back
        grad[3] = flow_grad
        gat[r, me_r] = flow_grad
        region_send(
            lambda k: gat.at[r, me_r],
            lambda k: gat.at[r, me_r],
            send_g.at[it],
            recv_g.at[it],
        )
        next_wait(4 + r)
        prev_grad = nb_dst[4 + r] + ys[0, 0:1, :]

        pltpu.make_async_copy(sbuf.at[r], sbuf.at[r], recv_r.at[r]).wait()
        sums = mr[r]
        for k in range(nr - 1):
            sums = sums + sbuf[r, k]
        total_p = jnp.sum(jnp.where(lane_low, sums, 0.0), axis=1, keepdims=True)
        total_d = jnp.sum(jnp.where(lane_low, 0.0, sums), axis=1, keepdims=True)
        total_p = jnp.broadcast_to(total_p, (1, LANES))
        total_d = jnp.broadcast_to(total_d, (1, LANES))
        weight = jnp.sqrt(
            weight
            * jnp.sqrt(total_p / primal_count + EPSILON)
            / jnp.sqrt(total_d / dual_count + EPSILON)
        )
        primal_step = STEP_SCALE / weight
        dual_step = STEP_SCALE * weight

        def primal(c, a):
            bar, sq = primal_block(c, xs[c], grad[c], primal_step)
            return bar, a + fold(sq)

        bar0, sq_p = primal(0, zero8)
        sq_p = unrolled(1, cb, 6, lambda c, a: primal(c, a)[1], sq_p)
        new_cap = jnp.maximum(cap - primal_step * (build - capacity_grad), 0.0)
        cap_diff = new_cap - cap
        prev_new = jnp.maximum(prev_x - primal_step * prev_grad, 0.0)
        prev_bar = prev_new + (prev_new - prev_x)

        def flow():
            pltpu.make_async_copy(
                gat.at[r, pl.ds(0, nr - 1)], gat.at[r, pl.ds(0, nr - 1)], recv_g.at[it]
            ).wait()
            line_grad = line_apply(lambda q: gat[r, q])
            new_line = line_a[...] - primal_step * line_grad
            line_a[...] = new_line
            return new_line - primal_step * line_grad

        sq_d = forward(bar0, prev_bar, lambda: new_cap + cap_diff, flow, dual_step, False)
        return prev_new, new_cap, cap_diff * cap_diff, weight, sq_p, sq_d

    first_diff = cap_new - cap_old
    carry = (
        prev_new,
        cap_new,
        first_diff * first_diff,
        jnp.ones((1, LANES), F32),
        sq_p,
        sq_d,
    )
    carry = lax.fori_loop(1, ITERS, later, carry)
    cap_out[...] = pltpu.roll(carry[1], lax.rem(LANES - me_t * own_n, LANES), 1)

    for r in range(ITERS):
        pltpu.make_async_copy(tbuf.at[r], tbuf.at[r], send_t.at[r]).wait()
    pltpu.make_async_copy(
        gat0.at[pl.ds(0, nr - 1)], gat0.at[pl.ds(0, nr - 1)], send_g.at[0]
    ).wait()
    for r in range(ITERS - 1):
        pltpu.make_async_copy(sbuf.at[r], sbuf.at[r], send_r.at[r]).wait()
        pltpu.make_async_copy(rbuf.at[r], rbuf.at[r], send_p.at[r]).wait()
        pltpu.make_async_copy(
            gat.at[r, pl.ds(0, nr - 1)], gat.at[r, pl.ds(0, nr - 1)], send_g.at[r + 1]
        ).wait()
    for n in range(1 + 2 * (ITERS - 1)):
        pltpu.make_async_copy(nb_src.at[n], nb_src.at[n], send_n.at[n]).wait()


def by_hour(x, y, cap, own):
    cb, hours, _, bs = x.shape

    def place(x_ref, y_ref, cap_ref, x_out, y_out, cap_out, sem):
        copies = []
        for c in range(cb):
            at = pl.ds(c * bs, bs)
            copies.append(pltpu.make_async_copy(x_ref.at[c], x_out.at[:, :, at], sem.at[0, c]))
            copies.append(pltpu.make_async_copy(y_ref.at[c], y_out.at[:, :, at], sem.at[1, c]))
        for copy in copies:
            copy.start()
        cap_out[...] = cap_ref[:, 0:own]
        for copy in copies:
            copy.wait()

    vmem = pl.BlockSpec(memory_space=pltpu.VMEM)
    hbm = pl.BlockSpec(memory_space=pl.ANY)
    shape = jax.ShapeDtypeStruct((hours, 1, cb * bs), F32)
    return pl.pallas_call(
        place,
        in_specs=[vmem, vmem, vmem],
        out_specs=(hbm, hbm, vmem),
        out_shape=(shape, shape, jax.ShapeDtypeStruct((1, own), F32)),
        scratch_shapes=[pltpu.SemaphoreType.DMA((2, cb))],
        compiler_params=pltpu.CompilerParams(vmem_limit_bytes=8 * 2**20),
    )(x, y, cap)


def in_hbm(value):
    return pltpu.with_memory_space_constraint(value, pltpu.HBM)


def body(
    start_primal,
    demand,
    unit_cost,
    build_cost,
    start_capacity,
    net_weights,
    net_columns,
    line_weights,
    line_source,
    generator_map,
):
    hours, _, width = start_primal.shape
    bs = net_weights.shape[3]
    cb = width // bs
    s_count = net_weights.shape[2]
    nl = line_weights.shape[1]
    nt = lax.axis_size("tm")
    nr = lax.axis_size("region")
    pairs = cb * s_count
    sizes = (hours, cb, bs, s_count, nl, nt, nr)
    smem = pl.BlockSpec(memory_space=pltpu.SMEM)
    vmem = pl.BlockSpec(memory_space=pltpu.VMEM)
    hbm = pl.BlockSpec(memory_space=pltpu.HBM)
    rounds = ITERS - 1
    dma = pltpu.SemaphoreType.DMA
    x_new, y_new, cap = pl.pallas_call(
        functools.partial(kernel, sizes),
        out_shape=(
            jax.ShapeDtypeStruct((cb, hours, bs), F32),
            jax.ShapeDtypeStruct((cb, hours, bs), F32),
            jax.ShapeDtypeStruct((1, LANES), F32),
        ),
        in_specs=[smem] * 4 + [vmem] * 2 + [hbm] * 4,
        out_specs=(vmem, vmem, vmem),
        scratch_shapes=[
            pltpu.VMEM((hours * cb, bs), F32),
            pltpu.VMEM((hours * cb, bs), F32),
            pltpu.VMEM((cb, s_count, bs, bs), F32),
            pltpu.VMEM((nl * bs, bs), F32),
            pltpu.VMEM((nl * bs, bs), BF16),
            pltpu.VMEM((nl * bs, bs), BF16),
            pltpu.VMEM((pairs, bs, bs), BF16),
            pltpu.VMEM((pairs, bs, bs), BF16),
            pltpu.VMEM((cb, hours, bs), F32),
            pltpu.VMEM((cb, hours, bs), F32),
            pltpu.VMEM((cb, 2 * hours, bs), BF16),
            pltpu.VMEM((cb, 2 * hours, bs), BF16),
            pltpu.VMEM((pairs, hours, bs), F32),
            pltpu.VMEM((3, hours, bs), F32),
            pltpu.VMEM((8, LANES), jnp.int32),
            pltpu.SMEM((8, LANES), jnp.int32),
            pltpu.VMEM((1, LANES), jnp.int32),
            pltpu.SMEM((1, LANES), jnp.int32),
            pltpu.VMEM((hours, bs), F32),
            pltpu.VMEM((8, bs), F32),
            pltpu.VMEM((hours + 8, bs), F32),
            pltpu.VMEM((nr, hours + 8, bs), F32),
            pltpu.VMEM((rounds, nr, hours, bs), F32),
            pltpu.VMEM((rounds, nr, hours, bs), F32),
            pltpu.VMEM((rounds, nr - 1, hours, bs), F32),
            pltpu.VMEM((ITERS, 1, 2 * LANES), F32),
            pltpu.VMEM((ITERS, nt - 1, 1, 2 * LANES), F32),
            pltpu.VMEM((rounds, 1, LANES), F32),
            pltpu.VMEM((rounds, nr - 1, 1, LANES), F32),
            pltpu.VMEM((1 + 2 * rounds, 1, LANES), F32),
            pltpu.VMEM((1 + 2 * rounds, 1, LANES), F32),
            dma((5,)),
            dma((cb,)),
            dma((ITERS,)),
            dma((ITERS,)),
            dma((rounds,)),
            dma((rounds,)),
            dma((ITERS,)),
            dma((ITERS,)),
            dma((rounds,)),
            dma((rounds,)),
            dma((1 + 2 * rounds,)),
            dma((1 + 2 * rounds,)),
        ],
        compiler_params=pltpu.CompilerParams(
            collective_id=0, has_side_effects=True, vmem_limit_bytes=40 * 2**20
        ),
    )(*(in_hbm(v) for v in (
        jnp.transpose(net_columns, (2, 0, 1)),
        jnp.transpose(line_source),
        start_capacity,
        build_cost,
        generator_map,
        unit_cost.reshape(cb, 1, bs),
        start_primal.reshape(hours * cb, bs),
        demand.reshape(hours * cb, bs),
        net_weights[0],
        line_weights.reshape(nl * bs, bs),
    )))
    parts = (cb, hours, 1, bs)
    return by_hour(x_new.reshape(parts), y_new.reshape(parts), cap, start_capacity.shape[1])


def solution(mesh):
    in_specs = (
        P("tm", "region", None),
        P("tm", "region", None),
        P("region", None),
        P("region", "tm"),
        P("region", "tm"),
        P("region", None, None, None, None),
        P("region", None, None),
        P("region", None, None, None),
        P(),
        P("region", None),
    )
    out_specs = (P("tm", "region", None), P("tm", "region", None), P("region", "tm"))
    return jax.shard_map(body, mesh=mesh, in_specs=in_specs, out_specs=out_specs, check_vma=False)
```

```python
import functools
import math

import jax
import jax.numpy as jnp
from jax import lax
from jax.experimental import pallas as pl
from jax.experimental.pallas import tpu as pltpu
from jax.sharding import PartitionSpec as P

ITERS = 4
STEP_SCALE = 0.2
EPSILON = 1e-06
HIGHEST = lax.Precision.HIGHEST
MESH = pl.DeviceIdType.MESH
F32 = jnp.float32
BF16 = jnp.bfloat16
LOW = float(jnp.finfo(jnp.float32).min)
LANES = 128


def split(value):
    high = value.astype(BF16)
    low = (value - high.astype(F32)).astype(BF16)
    return jnp.concatenate([high, low], axis=0)


def unrolled(first, last, by, step, carry):
    assert (last - first) % by == 0

    def some(n, c):
        for k in range(by):
            c = step(first + n * by + k, c)
        return c

    return lax.fori_loop(0, (last - first) // by, some, carry)


def dot_nt(a, b, precision=None):
    return lax.dot_general(
        a, b, (((1,), (1,)), ((), ())), precision=precision, preferred_element_type=F32
    )


def kernel(
    sizes,
    cols_hbm,
    src_hbm,
    cap_hbm,
    build_hbm,
    gm_hbm,
    unit_hbm,
    x_hbm,
    dem_hbm,
    w_hbm,
    lw_hbm,
    xs,
    ys,
    cap_out,
    cols_s,
    src_s,
    cap_s,
    build_s,
    gm_v,
    unit_v,
    xst,
    dst,
    wst,
    lw,
    lwh,
    lwl,
    wh,
    wl,
    tgt,
    grad,
    xb,
    yb,
    seg,
    extra,
    table_v,
    table_s,
    rank_v,
    rank_s,
    line_a,
    line_u,
    vx,
    gat0,
    gat,
    pbuf,
    rbuf,
    mt,
    tbuf,
    mr,
    sbuf,
    nb_src,
    nb_dst,
    load_sem,
    w_sem,
    send_t,
    recv_t,
    send_r,
    recv_r,
    send_g,
    recv_g,
    send_p,
    recv_p,
    send_n,
    recv_n,
):
    (hours, cb, bs, s_count, nl, nt, nr) = sizes
    pairs = cb * s_count
    me_t = lax.axis_index("tm")
    me_r = lax.axis_index("region")
    primal_count = hours * nt * nr * cb * bs + nr * LANES
    dual_count = hours * nt * nr * cb * bs
    couple = 1.0 / math.sqrt(hours * nt)

    cx = pltpu.make_async_copy(x_hbm, xst, load_sem.at[0])
    cu = pltpu.make_async_copy(unit_hbm, unit_v, load_sem.at[5])
    cc = pltpu.make_async_copy(cap_hbm, cap_s, load_sem.at[6])
    cbuild = pltpu.make_async_copy(build_hbm, build_s, load_sem.at[7])
    ck = pltpu.make_async_copy(cols_hbm, cols_s, load_sem.at[8])
    cs = pltpu.make_async_copy(src_hbm, src_s, load_sem.at[9])
    cg = pltpu.make_async_copy(gm_hbm, gm_v, load_sem.at[10])
    cd = pltpu.make_async_copy(dem_hbm, dst, load_sem.at[1])
    cl = pltpu.make_async_copy(lw_hbm, lw, load_sem.at[2])
    for c in (cx, cu, cc, cbuild):
        c.start()

    barrier = pltpu.get_barrier_semaphore()

    def offset_of(step, count):
        k = step + count // 2
        return jnp.where(k >= count, k - (count - 1), k)

    def around(me, k, count):
        at = me + k
        return jnp.where(at >= count, at - count, at)

    nx = 4 if nt % 4 == 0 else 1
    nz = nt // nx
    me_z, me_x = me_t // nx, me_t % nx

    def tm_partners(act):
        order = [(dz, dx) for dz in range(nz) for dx in range(nx) if dz or dx]
        order.sort(key=lambda d: -min(d[0], nz - d[0]) - min(d[1], nx - d[1]))
        for dz, dx in order:
            act(dz * nx + dx - 1, around(me_z, dz, nz) * nx + around(me_x, dx, nx))

    tm_partners(
        lambda slot, at: pl.semaphore_signal(
            barrier, inc=1, device_id=(at, me_r), device_id_type=MESH
        )
    )

    @pl.loop(0, nr - 1)
    def _(step):
        k = offset_of(step, nr)
        pl.semaphore_signal(
            barrier, inc=1, device_id=(me_t, around(me_r, k, nr)), device_id_type=MESH
        )

    for c in (ck, cs, cg, cd, cl):
        c.start()
    w_copies = [
        pltpu.make_async_copy(w_hbm.at[i], wst.at[i], w_sem.at[i]) for i in range(cb)
    ]
    for c in w_copies:
        c.start()

    lane = lax.broadcasted_iota(jnp.int32, (1, LANES), 1)

    own_n = LANES // nt
    cc.wait()
    cbuild.wait()
    cap_vec = jnp.zeros((1, LANES), F32)
    build_vec = jnp.zeros((1, LANES), F32)
    for k in range(own_n):
        here = lane == me_t * own_n + k
        cap_vec = jnp.where(here, cap_s[0, k], cap_vec)
        build_vec = jnp.where(here, build_s[0, k], build_vec)
    mt[0, :, 0:LANES] = cap_vec
    mt[0, :, LANES : 2 * LANES] = build_vec

    cx.wait()
    cu.wait()
    vx[0:hours, :] = xst[pl.ds(3, hours, stride=cb), :]
    vx[hours : hours + 8, :] = jnp.broadcast_to(unit_v[3], (8, LANES))
    nb_src[0] = xst[pl.ds((hours - 1) * cb, 1), :]

    pl.semaphore_wait(barrier, nt - 1 + nr - 1)

    def tm_send(r):
        def send(slot, at):
            pltpu.make_async_remote_copy(
                src_ref=mt.at[r],
                dst_ref=tbuf.at[r, slot],
                send_sem=send_t.at[r],
                recv_sem=recv_t.at[r],
                device_id=(at, me_r),
                device_id_type=MESH,
            ).start()

        tm_partners(send)

    def tm_sum(r):
        pltpu.make_async_copy(tbuf.at[r], tbuf.at[r], recv_t.at[r]).wait()
        total = mt[r]
        for k in range(nt - 1):
            total = total + tbuf[r, k]
        return total

    def region_send(src, dst_of, send_sem, recv_sem):
        @pl.loop(0, nr - 1)
        def _(step):
            k = offset_of(step, nr)
            pltpu.make_async_remote_copy(
                src_ref=src(k),
                dst_ref=dst_of(k),
                send_sem=send_sem,
                recv_sem=recv_sem,
                device_id=(me_t, around(me_r, k, nr)),
                device_id_type=MESH,
            ).start()

    def to_next(n, r, by):
        pltpu.make_async_remote_copy(
            src_ref=nb_src.at[n],
            dst_ref=nb_dst.at[n],
            send_sem=send_n.at[n],
            recv_sem=recv_n.at[n],
            device_id=(around(me_t, (by + nt) % nt, nt), me_r),
            device_id_type=MESH,
        ).start()

    def next_wait(n):
        pltpu.make_async_copy(nb_dst.at[n], nb_dst.at[n], recv_n.at[n]).wait()

    tm_send(0)
    region_send(
        lambda k: vx, lambda k: gat0.at[me_r], send_g.at[0], recv_g.at[0]
    )
    to_next(0, 0, 1)
    gat0[me_r] = vx[...]

    ck.wait()
    cs.wait()
    cg.wait()


    def column(p):
        return cols_s[p % s_count, 0, p // s_count]

    col_vec = jnp.full((1, LANES), cb, jnp.int32)
    for p in range(pairs):
        col_vec = jnp.where(lane == p, column(p), col_vec)
    rank = jnp.zeros((1, LANES), jnp.int32)
    end_vec = jnp.zeros((1, LANES), jnp.int32)
    for q in range(pairs):
        c = column(q)
        ahead = (col_vec > c) | ((col_vec == c) & (lane > q))
        rank = rank + jnp.where(ahead, 1, 0)
        end_vec = end_vec + jnp.where(lane >= c, 1, 0)
    start_vec = jnp.where(lane == 0, 0, pltpu.roll(end_vec, 1, 1))
    rank_v[...] = rank
    c1 = pltpu.make_async_copy(rank_v, rank_s, load_sem.at[3])
    c1.start()

    sel_t = jnp.where(
        gm_v[...] == lax.broadcasted_iota(jnp.int32, (LANES, LANES), 0), 1.0, 0.0
    ).astype(F32)

    c1.wait()
    order = jnp.zeros((1, LANES), jnp.int32)
    order_row = jnp.zeros((1, LANES), jnp.int32)
    order_col = jnp.full((1, LANES), -1, jnp.int32)
    for p in range(pairs):
        here = lane == rank_s[0, p]
        order = jnp.where(here, p, order)
        order_row = jnp.where(here, p // s_count, order_row)
        order_col = jnp.where(here, column(p), order_col)
    goes_on = (order_col == pltpu.roll(order_col, 1, 1)) & (lane > 0)
    table_v[0:1, :] = order
    table_v[1:2, :] = order_row
    table_v[2:3, :] = jnp.where(goes_on, 1, 0)
    table_v[3:4, :] = jnp.maximum(end_vec - 1, 0)
    table_v[4:5, :] = jnp.where(end_vec > start_vec, 1, 0)
    table_v[5:8, :] = jnp.zeros((3, LANES), jnp.int32)
    c2 = pltpu.make_async_copy(table_v, table_s, load_sem.at[4])
    c2.start()

    def split_weights(i):
        w_copies[i].wait()

        @pl.loop(0, s_count)
        def _(s):
            w = wst[i, s]
            high = w.astype(BF16)
            wh[i * s_count + s] = high
            wl[i * s_count + s] = (w - high.astype(F32)).astype(BF16)

    for i in range(cb):
        split_weights(i)

    cd.wait()
    cl.wait()

    def place_target(i, _):
        tgt[i] = dst[pl.ds(i, hours, stride=cb), :]
        return 0

    unrolled(0, cb, 5, place_target, 0)
    line_high = lw[...].astype(BF16)
    lwh[...] = line_high
    lwl[...] = (lw[...] - line_high.astype(F32)).astype(BF16)

    def primal_block(c, x, g, step):
        low = jnp.where(c == 3, LOW, 0.0)
        new = jnp.maximum(x - step * g, low)
        change = new - x
        bar = new + change
        xs[c] = new
        xb[c] = split(bar)
        return bar, change * change

    def fold(sq):
        return jnp.sum(sq.reshape(hours // 8, 8, LANES), axis=0)

    first_step = STEP_SCALE

    def first_primal(c, acc):
        x = xst[pl.ds(c, hours, stride=cb), :]
        g = jnp.broadcast_to(unit_v[c], (hours, LANES))
        bar, sq = primal_block(c, x, g, first_step)
        return bar, acc + fold(sq)

    zero8 = jnp.zeros((8, LANES), F32)
    bar0, sq_p = first_primal(0, zero8)
    sq_p = unrolled(1, cb, 4, lambda c, a: first_primal(c, a)[1], sq_p)

    def network(i):
        x3 = jnp.concatenate([xb[cols_s[s, 0, i]] for s in range(s_count)], axis=1)
        high = jnp.concatenate([wh[i * s_count + s] for s in range(s_count)], axis=0)
        low = jnp.concatenate([wl[i * s_count + s] for s in range(s_count)], axis=0)
        both = jnp.dot(x3, high, preferred_element_type=F32)
        last = jnp.dot(x3[0:hours], low, preferred_element_type=F32)
        return both[0:hours] + both[hours:] + last

    def dual_block(i, rest, step, first):
        low = jnp.where(i < 3, LOW, 0.0)
        move = step * rest
        if first:
            new = jnp.maximum(move, low)
            change = new
        else:
            old = ys[i]
            new = jnp.maximum(old + move, low)
            change = new - old
        ys[i] = new
        yb[i] = split(new)
        return fold(change * change)

    def target_of(i):
        return dst[pl.ds(i, hours, stride=cb), :]

    def line_apply(block_of):
        parts = jnp.concatenate([block_of(src_s[j, me_r]) for j in range(nl)], axis=1)
        high = parts.astype(BF16)
        low = (parts - high.astype(F32)).astype(BF16)
        return (
            jnp.dot(high, lwh[...], preferred_element_type=F32)
            + jnp.dot(low, lwh[...], preferred_element_type=F32)
            + jnp.dot(high, lwl[...], preferred_element_type=F32)
        )

    row = lax.broadcasted_iota(jnp.int32, (hours, LANES), 0)
    has_before = jnp.where(me_t > 0, 1.0, 0.0).astype(F32)
    has_after = jnp.where(me_t < nt - 1, 1.0, 0.0).astype(F32)

    def forward(bar0, prev_bar, cap_bar, line_flow, step, first):
        earlier = pltpu.roll(bar0, 1, 0)
        earlier = jnp.where(row == 0, prev_bar * has_before, earlier)
        tgt[0] = target_of(0) + earlier
        picked = jnp.dot(
            jnp.broadcast_to(cap_bar(), (8, LANES)),
            sel_t,
            precision=HIGHEST,
            preferred_element_type=F32,
        )[0:1]
        tgt[2] = target_of(2) - couple * picked
        tgt[1] = target_of(1) - network(1)

        def plain(n, a):
            i = jnp.where(n > 0, n + 1, 0)
            return a + dual_block(i, tgt[i] - network(i), step, first)

        sq = unrolled(0, cb - 1, 12, plain, zero8)
        return sq + dual_block(1, tgt[1] - line_flow(), step, first)

    lane_low = lane < LANES // 2

    def pack(p, d):
        p = jnp.sum(p, axis=0, keepdims=True)
        d = jnp.sum(d, axis=0, keepdims=True)
        p = p + pltpu.roll(p, LANES // 2, 1)
        d = d + pltpu.roll(d, LANES // 2, 1)
        return jnp.where(lane_low, p, d)

    gathered = []

    def first_capacity():
        total = tm_sum(0)
        cap = total[:, 0:LANES]
        build = total[:, LANES : 2 * LANES]
        new_cap = jnp.maximum(cap - first_step * build, 0.0)
        gathered.extend([cap, build, new_cap])
        return new_cap + (new_cap - cap)

    def first_flow():
        pltpu.make_async_copy(
            gat0.at[pl.ds(0, nr - 1)], gat0.at[pl.ds(0, nr - 1)], recv_g.at[0]
        ).wait()
        both = line_apply(lambda q: gat0[q])
        line_unit = both[hours : hours + 1]
        line_x = both[0:hours]
        line_u[...] = jnp.broadcast_to(line_unit, (8, LANES))
        new_line = line_x - first_step * line_unit
        line_a[...] = new_line
        return new_line - first_step * line_unit

    next_wait(0)
    prev_old = nb_dst[0]
    prev_new = jnp.maximum(prev_old - first_step * unit_v[0], 0.0)
    prev_bar = prev_new + (prev_new - prev_old)
    sq_d = forward(bar0, prev_bar, first_capacity, first_flow, first_step, True)
    cap_old, build, cap_new = gathered

    c2.wait()

    def later(it, carry):
        prev_x, cap, cap_change, weight, sq_p, sq_d = carry
        r = it - 1
        mt[it, :, 0:LANES] = jnp.sum(ys[2], axis=0, keepdims=True)
        mt[it, :, LANES : 2 * LANES] = pack(sq_p, sq_d)
        nb_src[1 + r] = ys[0, 0:1, :]
        tm_send(it)
        to_next(1 + r, r, -1)

        y1 = yb[1]
        terms = (
            dot_nt(y1[0:hours], lwh[...])
            + dot_nt(y1[hours:], lwh[...])
            + dot_nt(y1[0:hours], lwl[...])
        )
        for k in range(nr):
            q = around(me_r, k, nr)
            total = jnp.zeros((hours, LANES), F32)
            for j in range(nl):
                on = jnp.where(src_s[j, me_r] == q, 1.0, 0.0).astype(F32)
                total = total + on * terms[:, j * bs : (j + 1) * bs]
            pbuf[r, k] = total
        region_send(
            lambda k: pbuf.at[r, k], lambda k: rbuf.at[r, k - 1], send_p.at[r], recv_p.at[r]
        )

        def pair(n, total):
            p = table_s[0, n]
            y = yb[table_s[1, n]]
            keep = table_s[2, n].astype(F32)
            both = dot_nt(y, wh[p])
            low = dot_nt(y[0:hours], wl[p])
            total = keep * total + (both[0:hours] + both[hours:] + low)
            seg[n] = total
            return total

        unrolled(0, pairs, 15, pair, jnp.zeros((hours, LANES), F32))

        def gradient(c, _):
            grad[c] = unit_v[c] - table_s[4, c].astype(F32) * seg[table_s[3, c]]
            return 0

        unrolled(0, cb, 5, gradient, 0)
        nb_src[4 + r] = grad[0, hours - 1 : hours, :]
        to_next(4 + r, r, 1)

        next_wait(1 + r)
        following = pltpu.roll(ys[0], hours - 1, 0)
        following = jnp.where(row == hours - 1, nb_dst[1 + r] * has_after, following)
        grad[0] = grad[0] + following

        total = tm_sum(it)
        col_sums = total[:, 0:LANES]
        region_sums = total[:, LANES : 2 * LANES] + pack(
            cap_change, jnp.zeros_like(cap_change)
        )
        mr[r] = region_sums
        region_send(
            lambda k: mr.at[r], lambda k: sbuf.at[r, k - 1], send_r.at[r], recv_r.at[r]
        )
        capacity_grad = couple * dot_nt(
            jnp.broadcast_to(col_sums, (8, LANES)), sel_t, precision=HIGHEST
        )[0:1]

        pltpu.make_async_copy(rbuf.at[r], rbuf.at[r], recv_p.at[r]).wait()
        line_back = pbuf[r, 0]
        for k in range(nr - 1):
            line_back = line_back + rbuf[r, k]
        flow_grad = grad[3] - line_back
        grad[3] = flow_grad
        gat[r, me_r] = flow_grad
        region_send(
            lambda k: gat.at[r, me_r],
            lambda k: gat.at[r, me_r],
            send_g.at[it],
            recv_g.at[it],
        )
        next_wait(4 + r)
        prev_grad = nb_dst[4 + r] + ys[0, 0:1, :]

        pltpu.make_async_copy(sbuf.at[r], sbuf.at[r], recv_r.at[r]).wait()
        sums = mr[r]
        for k in range(nr - 1):
            sums = sums + sbuf[r, k]
        total_p = jnp.sum(jnp.where(lane_low, sums, 0.0), axis=1, keepdims=True)
        total_d = jnp.sum(jnp.where(lane_low, 0.0, sums), axis=1, keepdims=True)
        total_p = jnp.broadcast_to(total_p, (1, LANES))
        total_d = jnp.broadcast_to(total_d, (1, LANES))
        weight = jnp.sqrt(
            weight
            * jnp.sqrt(total_p / primal_count + EPSILON)
            / jnp.sqrt(total_d / dual_count + EPSILON)
        )
        primal_step = STEP_SCALE / weight
        dual_step = STEP_SCALE * weight

        def primal(c, a):
            bar, sq = primal_block(c, xs[c], grad[c], primal_step)
            return bar, a + fold(sq)

        bar0, sq_p = primal(0, zero8)
        sq_p = unrolled(1, cb, 6, lambda c, a: primal(c, a)[1], sq_p)
        new_cap = jnp.maximum(cap - primal_step * (build - capacity_grad), 0.0)
        cap_diff = new_cap - cap
        prev_new = jnp.maximum(prev_x - primal_step * prev_grad, 0.0)
        prev_bar = prev_new + (prev_new - prev_x)

        def flow():
            pltpu.make_async_copy(
                gat.at[r, pl.ds(0, nr - 1)], gat.at[r, pl.ds(0, nr - 1)], recv_g.at[it]
            ).wait()
            line_grad = line_apply(lambda q: gat[r, q])
            new_line = line_a[...] - primal_step * line_grad
            line_a[...] = new_line
            return new_line - primal_step * line_grad

        sq_d = forward(bar0, prev_bar, lambda: new_cap + cap_diff, flow, dual_step, False)
        return prev_new, new_cap, cap_diff * cap_diff, weight, sq_p, sq_d

    first_diff = cap_new - cap_old
    carry = (
        prev_new,
        cap_new,
        first_diff * first_diff,
        jnp.ones((1, LANES), F32),
        sq_p,
        sq_d,
    )
    carry = lax.fori_loop(1, ITERS, later, carry)
    cap_out[...] = pltpu.roll(carry[1], lax.rem(LANES - me_t * own_n, LANES), 1)

    for r in range(ITERS):
        pltpu.make_async_copy(tbuf.at[r], tbuf.at[r], send_t.at[r]).wait()
    pltpu.make_async_copy(
        gat0.at[pl.ds(0, nr - 1)], gat0.at[pl.ds(0, nr - 1)], send_g.at[0]
    ).wait()
    for r in range(ITERS - 1):
        pltpu.make_async_copy(sbuf.at[r], sbuf.at[r], send_r.at[r]).wait()
        pltpu.make_async_copy(rbuf.at[r], rbuf.at[r], send_p.at[r]).wait()
        pltpu.make_async_copy(
            gat.at[r, pl.ds(0, nr - 1)], gat.at[r, pl.ds(0, nr - 1)], send_g.at[r + 1]
        ).wait()
    for n in range(1 + 2 * (ITERS - 1)):
        pltpu.make_async_copy(nb_src.at[n], nb_src.at[n], send_n.at[n]).wait()


def by_hour(x, y, cap, own):
    cb, hours, _, bs = x.shape

    def place(x_ref, y_ref, cap_ref, x_out, y_out, cap_out, sem):
        copies = []
        for c in range(cb):
            at = pl.ds(c * bs, bs)
            copies.append(pltpu.make_async_copy(x_ref.at[c], x_out.at[:, :, at], sem.at[0, c]))
            copies.append(pltpu.make_async_copy(y_ref.at[c], y_out.at[:, :, at], sem.at[1, c]))
        for copy in copies:
            copy.start()
        cap_out[...] = cap_ref[:, 0:own]
        for copy in copies:
            copy.wait()

    vmem = pl.BlockSpec(memory_space=pltpu.VMEM)
    hbm = pl.BlockSpec(memory_space=pl.ANY)
    shape = jax.ShapeDtypeStruct((hours, 1, cb * bs), F32)
    return pl.pallas_call(
        place,
        in_specs=[vmem, vmem, vmem],
        out_specs=(hbm, hbm, vmem),
        out_shape=(shape, shape, jax.ShapeDtypeStruct((1, own), F32)),
        scratch_shapes=[pltpu.SemaphoreType.DMA((2, cb))],
        compiler_params=pltpu.CompilerParams(vmem_limit_bytes=8 * 2**20),
    )(x, y, cap)


def in_hbm(value):
    return pltpu.with_memory_space_constraint(value, pltpu.HBM)


def body(
    start_primal,
    demand,
    unit_cost,
    build_cost,
    start_capacity,
    net_weights,
    net_columns,
    line_weights,
    line_source,
    generator_map,
):
    hours, _, width = start_primal.shape
    bs = net_weights.shape[3]
    cb = width // bs
    s_count = net_weights.shape[2]
    nl = line_weights.shape[1]
    nt = lax.axis_size("tm")
    nr = lax.axis_size("region")
    pairs = cb * s_count
    sizes = (hours, cb, bs, s_count, nl, nt, nr)
    vmem = pl.BlockSpec(memory_space=pltpu.VMEM)
    hbm = pl.BlockSpec(memory_space=pltpu.HBM)
    rounds = ITERS - 1
    dma = pltpu.SemaphoreType.DMA
    x_new, y_new, cap = pl.pallas_call(
        functools.partial(kernel, sizes),
        out_shape=(
            jax.ShapeDtypeStruct((cb, hours, bs), F32),
            jax.ShapeDtypeStruct((cb, hours, bs), F32),
            jax.ShapeDtypeStruct((1, LANES), F32),
        ),
        in_specs=[hbm] * 10,
        out_specs=(vmem, vmem, vmem),
        scratch_shapes=[
            pltpu.SMEM((s_count, 1, cb), jnp.int32),
            pltpu.SMEM(line_source.shape[::-1], jnp.int32),
            pltpu.SMEM(start_capacity.shape, F32),
            pltpu.SMEM(build_cost.shape, F32),
            pltpu.VMEM(generator_map.shape, jnp.int32),
            pltpu.VMEM((cb, 1, bs), F32),
            pltpu.VMEM((hours * cb, bs), F32),
            pltpu.VMEM((hours * cb, bs), F32),
            pltpu.VMEM((cb, s_count, bs, bs), F32),
            pltpu.VMEM((nl * bs, bs), F32),
            pltpu.VMEM((nl * bs, bs), BF16),
            pltpu.VMEM((nl * bs, bs), BF16),
            pltpu.VMEM((pairs, bs, bs), BF16),
            pltpu.VMEM((pairs, bs, bs), BF16),
            pltpu.VMEM((cb, hours, bs), F32),
            pltpu.VMEM((cb, hours, bs), F32),
            pltpu.VMEM((cb, 2 * hours, bs), BF16),
            pltpu.VMEM((cb, 2 * hours, bs), BF16),
            pltpu.VMEM((pairs, hours, bs), F32),
            pltpu.VMEM((3, hours, bs), F32),
            pltpu.VMEM((8, LANES), jnp.int32),
            pltpu.SMEM((8, LANES), jnp.int32),
            pltpu.VMEM((1, LANES), jnp.int32),
            pltpu.SMEM((1, LANES), jnp.int32),
            pltpu.VMEM((hours, bs), F32),
            pltpu.VMEM((8, bs), F32),
            pltpu.VMEM((hours + 8, bs), F32),
            pltpu.VMEM((nr, hours + 8, bs), F32),
            pltpu.VMEM((rounds, nr, hours, bs), F32),
            pltpu.VMEM((rounds, nr, hours, bs), F32),
            pltpu.VMEM((rounds, nr - 1, hours, bs), F32),
            pltpu.VMEM((ITERS, 1, 2 * LANES), F32),
            pltpu.VMEM((ITERS, nt - 1, 1, 2 * LANES), F32),
            pltpu.VMEM((rounds, 1, LANES), F32),
            pltpu.VMEM((rounds, nr - 1, 1, LANES), F32),
            pltpu.VMEM((1 + 2 * rounds, 1, LANES), F32),
            pltpu.VMEM((1 + 2 * rounds, 1, LANES), F32),
            dma((11,)),
            dma((cb,)),
            dma((ITERS,)),
            dma((ITERS,)),
            dma((rounds,)),
            dma((rounds,)),
            dma((ITERS,)),
            dma((ITERS,)),
            dma((rounds,)),
            dma((rounds,)),
            dma((1 + 2 * rounds,)),
            dma((1 + 2 * rounds,)),
        ],
        compiler_params=pltpu.CompilerParams(
            collective_id=0, has_side_effects=True, vmem_limit_bytes=40 * 2**20
        ),
    )(*(in_hbm(v) for v in (
        jnp.transpose(net_columns, (2, 0, 1)),
        jnp.transpose(line_source),
        start_capacity,
        build_cost,
        generator_map,
        unit_cost.reshape(cb, 1, bs),
        start_primal.reshape(hours * cb, bs),
        demand.reshape(hours * cb, bs),
        net_weights[0],
        line_weights.reshape(nl * bs, bs),
    )))
    parts = (cb, hours, 1, bs)
    return by_hour(x_new.reshape(parts), y_new.reshape(parts), cap, start_capacity.shape[1])


def solution(mesh):
    in_specs = (
        P("tm", "region", None),
        P("tm", "region", None),
        P("region", None),
        P("region", "tm"),
        P("region", "tm"),
        P("region", None, None, None, None),
        P("region", None, None),
        P("region", None, None, None),
        P(),
        P("region", None),
    )
    out_specs = (P("tm", "region", None), P("tm", "region", None), P("region", "tm"))
    return jax.shard_map(body, mesh=mesh, in_specs=in_specs, out_specs=out_specs, check_vma=False)
```

```python
import functools
import math

import jax
import jax.numpy as jnp
from jax import lax
from jax.experimental import pallas as pl
from jax.experimental.pallas import tpu as pltpu
from jax.sharding import PartitionSpec as P

ITERS = 4
STEP_SCALE = 0.2
EPSILON = 1e-06
HIGHEST = lax.Precision.HIGHEST
MESH = pl.DeviceIdType.MESH
F32 = jnp.float32
BF16 = jnp.bfloat16
LOW = float(jnp.finfo(jnp.float32).min)
LANES = 128


def split(value):
    high = value.astype(BF16)
    low = (value - high.astype(F32)).astype(BF16)
    return jnp.concatenate([high, low], axis=0)


def unrolled(first, last, by, step, carry):
    assert (last - first) % by == 0

    def some(n, c):
        for k in range(by):
            c = step(first + n * by + k, c)
        return c

    return lax.fori_loop(0, (last - first) // by, some, carry)


def dot_nt(a, b, precision=None):
    return lax.dot_general(
        a, b, (((1,), (1,)), ((), ())), precision=precision, preferred_element_type=F32
    )


def kernel(
    sizes,
    cols_hbm,
    src_hbm,
    cap_hbm,
    build_hbm,
    gm_hbm,
    unit_hbm,
    x_hbm,
    dem_hbm,
    w_hbm,
    lw_hbm,
    xs,
    ys,
    cap_out,
    cols_s,
    src_s,
    cap_s,
    build_s,
    gm_v,
    unit_v,
    xst,
    dst,
    wst,
    lw,
    lwh,
    lwl,
    wh,
    wl,
    tgt,
    grad,
    xb,
    yb,
    seg,
    extra,
    table_v,
    table_s,
    rank_v,
    rank_s,
    line_a,
    line_u,
    vx,
    gat0,
    gat,
    pbuf,
    rbuf,
    mt,
    tbuf,
    mr,
    sbuf,
    nb_src,
    nb_dst,
    load_sem,
    w_sem,
    send_t,
    recv_t,
    send_r,
    recv_r,
    send_g,
    recv_g,
    send_p,
    recv_p,
    send_n,
    recv_n,
):
    (hours, cb, bs, s_count, nl, nt, nr) = sizes
    pairs = cb * s_count
    me_t = lax.axis_index("tm")
    me_r = lax.axis_index("region")
    primal_count = hours * nt * nr * cb * bs + nr * LANES
    dual_count = hours * nt * nr * cb * bs
    couple = 1.0 / math.sqrt(hours * nt)

    cx = pltpu.make_async_copy(x_hbm, xst, load_sem.at[0])
    cu = pltpu.make_async_copy(unit_hbm, unit_v, load_sem.at[5])
    cc = pltpu.make_async_copy(cap_hbm, cap_s, load_sem.at[6])
    cbuild = pltpu.make_async_copy(build_hbm, build_s, load_sem.at[7])
    ck = pltpu.make_async_copy(cols_hbm, cols_s, load_sem.at[8])
    cs = pltpu.make_async_copy(src_hbm, src_s, load_sem.at[9])
    cg = pltpu.make_async_copy(gm_hbm, gm_v, load_sem.at[10])
    cd = pltpu.make_async_copy(dem_hbm, dst, load_sem.at[1])
    cl = pltpu.make_async_copy(lw_hbm, lw, load_sem.at[2])
    for c in (cx, cu, cc, cbuild):
        c.start()

    barrier = pltpu.get_barrier_semaphore()

    def offset_of(step, count):
        k = step + count // 2
        return jnp.where(k >= count, k - (count - 1), k)

    def around(me, k, count):
        at = me + k
        return jnp.where(at >= count, at - count, at)

    nx = 4 if nt % 4 == 0 else 1
    nz = nt // nx
    me_z, me_x = me_t // nx, me_t % nx

    def tm_partners(act):
        order = [(dz, dx) for dz in range(nz) for dx in range(nx) if dz or dx]
        order.sort(key=lambda d: -min(d[0], nz - d[0]) - min(d[1], nx - d[1]))
        for dz, dx in order:
            act(dz * nx + dx - 1, around(me_z, dz, nz) * nx + around(me_x, dx, nx))

    tm_partners(
        lambda slot, at: pl.semaphore_signal(
            barrier, inc=1, device_id=(at, me_r), device_id_type=MESH
        )
    )

    @pl.loop(0, nr - 1)
    def _(step):
        k = offset_of(step, nr)
        pl.semaphore_signal(
            barrier, inc=1, device_id=(me_t, around(me_r, k, nr)), device_id_type=MESH
        )

    for c in (ck, cs, cg, cd, cl):
        c.start()
    w_copies = [
        pltpu.make_async_copy(w_hbm.at[i], wst.at[i], w_sem.at[i]) for i in range(cb)
    ]
    for c in w_copies:
        c.start()

    lane = lax.broadcasted_iota(jnp.int32, (1, LANES), 1)

    own_n = LANES // nt
    cc.wait()
    cbuild.wait()
    cap_vec = jnp.zeros((1, LANES), F32)
    build_vec = jnp.zeros((1, LANES), F32)
    for k in range(own_n):
        here = lane == me_t * own_n + k
        cap_vec = jnp.where(here, cap_s[0, k], cap_vec)
        build_vec = jnp.where(here, build_s[0, k], build_vec)
    mt[0, :, 0:LANES] = cap_vec
    mt[0, :, LANES : 2 * LANES] = build_vec

    cx.wait()
    cu.wait()
    vx[0:hours, :] = xst[pl.ds(3, hours, stride=cb), :]
    vx[hours : hours + 8, :] = jnp.broadcast_to(unit_v[3], (8, LANES))
    nb_src[0] = xst[pl.ds((hours - 1) * cb, 1), :]

    pl.semaphore_wait(barrier, nt - 1 + nr - 1)

    def tm_send(r):
        def send(slot, at):
            pltpu.make_async_remote_copy(
                src_ref=mt.at[r],
                dst_ref=tbuf.at[r, slot],
                send_sem=send_t.at[r],
                recv_sem=recv_t.at[r],
                device_id=(at, me_r),
                device_id_type=MESH,
            ).start()

        tm_partners(send)

    def tm_sum(r):
        pltpu.make_async_copy(tbuf.at[r], tbuf.at[r], recv_t.at[r]).wait()
        parts = [mt[r]] + [tbuf[r, k] for k in range(nt - 1)]
        while len(parts) > 1:
            parts = [sum(parts[n + 1 : n + 2], parts[n]) for n in range(0, len(parts), 2)]
        return parts[0]

    def region_send(src, dst_of, send_sem, recv_sem):
        @pl.loop(0, nr - 1)
        def _(step):
            k = offset_of(step, nr)
            pltpu.make_async_remote_copy(
                src_ref=src(k),
                dst_ref=dst_of(k),
                send_sem=send_sem,
                recv_sem=recv_sem,
                device_id=(me_t, around(me_r, k, nr)),
                device_id_type=MESH,
            ).start()

    def to_next(n, r, by):
        pltpu.make_async_remote_copy(
            src_ref=nb_src.at[n],
            dst_ref=nb_dst.at[n],
            send_sem=send_n.at[n],
            recv_sem=recv_n.at[n],
            device_id=(around(me_t, (by + nt) % nt, nt), me_r),
            device_id_type=MESH,
        ).start()

    def next_wait(n):
        pltpu.make_async_copy(nb_dst.at[n], nb_dst.at[n], recv_n.at[n]).wait()

    tm_send(0)
    region_send(
        lambda k: vx, lambda k: gat0.at[me_r], send_g.at[0], recv_g.at[0]
    )
    to_next(0, 0, 1)
    gat0[me_r] = vx[...]

    ck.wait()
    cs.wait()
    cg.wait()


    def column(p):
        return cols_s[p % s_count, 0, p // s_count]

    col_vec = jnp.full((1, LANES), cb, jnp.int32)
    for p in range(pairs):
        col_vec = jnp.where(lane == p, column(p), col_vec)
    rank = jnp.zeros((1, LANES), jnp.int32)
    end_vec = jnp.zeros((1, LANES), jnp.int32)
    for q in range(pairs):
        c = column(q)
        ahead = (col_vec > c) | ((col_vec == c) & (lane > q))
        rank = rank + jnp.where(ahead, 1, 0)
        end_vec = end_vec + jnp.where(lane >= c, 1, 0)
    start_vec = jnp.where(lane == 0, 0, pltpu.roll(end_vec, 1, 1))
    rank_v[...] = rank
    c1 = pltpu.make_async_copy(rank_v, rank_s, load_sem.at[3])
    c1.start()

    sel_t = jnp.where(
        gm_v[...] == lax.broadcasted_iota(jnp.int32, (LANES, LANES), 0), 1.0, 0.0
    ).astype(F32)

    c1.wait()
    order = jnp.zeros((1, LANES), jnp.int32)
    order_row = jnp.zeros((1, LANES), jnp.int32)
    order_col = jnp.full((1, LANES), -1, jnp.int32)
    for p in range(pairs):
        here = lane == rank_s[0, p]
        order = jnp.where(here, p, order)
        order_row = jnp.where(here, p // s_count, order_row)
        order_col = jnp.where(here, column(p), order_col)
    goes_on = (order_col == pltpu.roll(order_col, 1, 1)) & (lane > 0)
    table_v[0:1, :] = order
    table_v[1:2, :] = order_row
    table_v[2:3, :] = jnp.where(goes_on, 1, 0)
    table_v[3:4, :] = jnp.maximum(end_vec - 1, 0)
    table_v[4:5, :] = jnp.where(end_vec > start_vec, 1, 0)
    table_v[5:8, :] = jnp.zeros((3, LANES), jnp.int32)
    c2 = pltpu.make_async_copy(table_v, table_s, load_sem.at[4])
    c2.start()

    def split_weights(i):
        w_copies[i].wait()

        @pl.loop(0, s_count)
        def _(s):
            w = wst[i, s]
            high = w.astype(BF16)
            wh[i * s_count + s] = high
            wl[i * s_count + s] = (w - high.astype(F32)).astype(BF16)

    for i in range(cb):
        split_weights(i)

    cd.wait()
    cl.wait()

    def place_target(i, _):
        tgt[i] = dst[pl.ds(i, hours, stride=cb), :]
        return 0

    unrolled(0, cb, 5, place_target, 0)
    line_high = lw[...].astype(BF16)
    lwh[...] = line_high
    lwl[...] = (lw[...] - line_high.astype(F32)).astype(BF16)

    def primal_block(c, x, g, step):
        low = jnp.where(c == 3, LOW, 0.0)
        new = jnp.maximum(x - step * g, low)
        change = new - x
        bar = new + change
        xs[c] = new
        xb[c] = split(bar)
        return bar, change * change

    def fold(sq):
        return jnp.sum(sq.reshape(hours // 8, 8, LANES), axis=0)

    first_step = STEP_SCALE

    def first_primal(c, acc):
        x = xst[pl.ds(c, hours, stride=cb), :]
        g = jnp.broadcast_to(unit_v[c], (hours, LANES))
        bar, sq = primal_block(c, x, g, first_step)
        return bar, acc + fold(sq)

    zero8 = jnp.zeros((8, LANES), F32)
    bar0, sq_p = first_primal(0, zero8)
    sq_p = unrolled(1, cb, 4, lambda c, a: first_primal(c, a)[1], sq_p)

    def network(i):
        x3 = jnp.concatenate([xb[cols_s[s, 0, i]] for s in range(s_count)], axis=1)
        high = jnp.concatenate([wh[i * s_count + s] for s in range(s_count)], axis=0)
        low = jnp.concatenate([wl[i * s_count + s] for s in range(s_count)], axis=0)
        both = jnp.dot(x3, high, preferred_element_type=F32)
        last = jnp.dot(x3[0:hours], low, preferred_element_type=F32)
        return both[0:hours] + both[hours:] + last

    def dual_block(i, rest, step, first):
        low = jnp.where(i < 3, LOW, 0.0)
        move = step * rest
        if first:
            new = jnp.maximum(move, low)
            change = new
        else:
            old = ys[i]
            new = jnp.maximum(old + move, low)
            change = new - old
        ys[i] = new
        yb[i] = split(new)
        return fold(change * change)

    def target_of(i):
        return dst[pl.ds(i, hours, stride=cb), :]

    def line_apply(block_of):
        parts = jnp.concatenate([block_of(src_s[j, me_r]) for j in range(nl)], axis=1)
        high = parts.astype(BF16)
        low = (parts - high.astype(F32)).astype(BF16)
        return (
            jnp.dot(high, lwh[...], preferred_element_type=F32)
            + jnp.dot(low, lwh[...], preferred_element_type=F32)
            + jnp.dot(high, lwl[...], preferred_element_type=F32)
        )

    row = lax.broadcasted_iota(jnp.int32, (hours, LANES), 0)
    has_before = jnp.where(me_t > 0, 1.0, 0.0).astype(F32)
    has_after = jnp.where(me_t < nt - 1, 1.0, 0.0).astype(F32)

    def forward(bar0, prev_bar, cap_bar, line_flow, step, first):
        earlier = pltpu.roll(bar0, 1, 0)
        earlier = jnp.where(row == 0, prev_bar * has_before, earlier)

        def capacity_term():
            return couple * jnp.dot(
                jnp.broadcast_to(cap_bar(), (8, LANES)),
                sel_t,
                precision=HIGHEST,
                preferred_element_type=F32,
            )[0:1]

        def plain(i, a):
            return a + dual_block(i, tgt[i] - network(i), step, first)

        if first:
            sq = unrolled(3, cb, 11, plain, zero8)
        else:
            picked = capacity_term()
            sq = zero8
            for i in range(3, cb):
                sq = plain(i, sq)
        sq = sq + dual_block(0, tgt[0] + earlier - network(0), step, first)
        rest = tgt[2] - network(2)
        last = tgt[1] - network(1)
        if first:
            picked = capacity_term()
        sq = sq + dual_block(2, rest - picked, step, first)
        return sq + dual_block(1, last - line_flow(), step, first)

    lane_low = lane < LANES // 2

    def pack(p, d):
        p = jnp.sum(p, axis=0, keepdims=True)
        d = jnp.sum(d, axis=0, keepdims=True)
        p = p + pltpu.roll(p, LANES // 2, 1)
        d = d + pltpu.roll(d, LANES // 2, 1)
        return jnp.where(lane_low, p, d)

    gathered = []

    def first_capacity():
        total = tm_sum(0)
        cap = total[:, 0:LANES]
        build = total[:, LANES : 2 * LANES]
        new_cap = jnp.maximum(cap - first_step * build, 0.0)
        gathered.extend([cap, build, new_cap])
        return new_cap + (new_cap - cap)

    def first_flow():
        pltpu.make_async_copy(
            gat0.at[pl.ds(0, nr - 1)], gat0.at[pl.ds(0, nr - 1)], recv_g.at[0]
        ).wait()
        both = line_apply(lambda q: gat0[q])
        line_unit = both[hours : hours + 1]
        line_x = both[0:hours]
        line_u[...] = jnp.broadcast_to(line_unit, (8, LANES))
        new_line = line_x - first_step * line_unit
        line_a[...] = new_line
        return new_line - first_step * line_unit

    next_wait(0)
    prev_old = nb_dst[0]
    prev_new = jnp.maximum(prev_old - first_step * unit_v[0], 0.0)
    prev_bar = prev_new + (prev_new - prev_old)
    sq_d = forward(bar0, prev_bar, first_capacity, first_flow, first_step, True)
    cap_old, build, cap_new = gathered

    c2.wait()

    def later(it, carry):
        prev_x, cap, cap_change, weight, sq_p, sq_d = carry
        r = it - 1
        mt[it, :, 0:LANES] = jnp.sum(ys[2], axis=0, keepdims=True)
        mt[it, :, LANES : 2 * LANES] = pack(sq_p, sq_d)
        nb_src[1 + r] = ys[0, 0:1, :]
        tm_send(it)
        to_next(1 + r, r, -1)

        y1 = yb[1]
        terms = (
            dot_nt(y1[0:hours], lwh[...])
            + dot_nt(y1[hours:], lwh[...])
            + dot_nt(y1[0:hours], lwl[...])
        )
        for k in range(nr):
            q = around(me_r, k, nr)
            total = jnp.zeros((hours, LANES), F32)
            for j in range(nl):
                on = jnp.where(src_s[j, me_r] == q, 1.0, 0.0).astype(F32)
                total = total + on * terms[:, j * bs : (j + 1) * bs]
            pbuf[r, k] = total
        region_send(
            lambda k: pbuf.at[r, k], lambda k: rbuf.at[r, k - 1], send_p.at[r], recv_p.at[r]
        )

        def pair(n, total):
            p = table_s[0, n]
            y = yb[table_s[1, n]]
            keep = table_s[2, n].astype(F32)
            both = dot_nt(y, wh[p])
            low = dot_nt(y[0:hours], wl[p])
            total = keep * total + (both[0:hours] + both[hours:] + low)
            seg[n] = total
            return total

        unrolled(0, pairs, 15, pair, jnp.zeros((hours, LANES), F32))

        def gradient(c, _):
            grad[c] = unit_v[c] - table_s[4, c].astype(F32) * seg[table_s[3, c]]
            return 0

        unrolled(0, cb, 5, gradient, 0)
        nb_src[4 + r] = grad[0, hours - 1 : hours, :]
        to_next(4 + r, r, 1)

        next_wait(1 + r)
        following = pltpu.roll(ys[0], hours - 1, 0)
        following = jnp.where(row == hours - 1, nb_dst[1 + r] * has_after, following)
        grad[0] = grad[0] + following

        total = tm_sum(it)
        col_sums = total[:, 0:LANES]
        region_sums = total[:, LANES : 2 * LANES] + pack(
            cap_change, jnp.zeros_like(cap_change)
        )
        mr[r] = region_sums
        region_send(
            lambda k: mr.at[r], lambda k: sbuf.at[r, k - 1], send_r.at[r], recv_r.at[r]
        )
        capacity_grad = couple * dot_nt(
            jnp.broadcast_to(col_sums, (8, LANES)), sel_t, precision=HIGHEST
        )[0:1]

        pltpu.make_async_copy(rbuf.at[r], rbuf.at[r], recv_p.at[r]).wait()
        line_back = pbuf[r, 0]
        for k in range(nr - 1):
            line_back = line_back + rbuf[r, k]
        flow_grad = grad[3] - line_back
        grad[3] = flow_grad
        gat[r, me_r] = flow_grad
        region_send(
            lambda k: gat.at[r, me_r],
            lambda k: gat.at[r, me_r],
            send_g.at[it],
            recv_g.at[it],
        )
        next_wait(4 + r)
        prev_grad = nb_dst[4 + r] + ys[0, 0:1, :]

        pltpu.make_async_copy(sbuf.at[r], sbuf.at[r], recv_r.at[r]).wait()
        sums = mr[r]
        for k in range(nr - 1):
            sums = sums + sbuf[r, k]
        total_p = jnp.sum(jnp.where(lane_low, sums, 0.0), axis=1, keepdims=True)
        total_d = jnp.sum(jnp.where(lane_low, 0.0, sums), axis=1, keepdims=True)
        total_p = jnp.broadcast_to(total_p, (1, LANES))
        total_d = jnp.broadcast_to(total_d, (1, LANES))
        weight = jnp.sqrt(
            weight
            * jnp.sqrt(total_p / primal_count + EPSILON)
            / jnp.sqrt(total_d / dual_count + EPSILON)
        )
        primal_step = STEP_SCALE / weight
        dual_step = STEP_SCALE * weight

        def primal(c, a):
            bar, sq = primal_block(c, xs[c], grad[c], primal_step)
            return bar, a + fold(sq)

        bar0, sq_p = primal(0, zero8)
        sq_p = unrolled(1, cb, 6, lambda c, a: primal(c, a)[1], sq_p)
        new_cap = jnp.maximum(cap - primal_step * (build - capacity_grad), 0.0)
        cap_diff = new_cap - cap
        prev_new = jnp.maximum(prev_x - primal_step * prev_grad, 0.0)
        prev_bar = prev_new + (prev_new - prev_x)

        def flow():
            pltpu.make_async_copy(
                gat.at[r, pl.ds(0, nr - 1)], gat.at[r, pl.ds(0, nr - 1)], recv_g.at[it]
            ).wait()
            line_grad = line_apply(lambda q: gat[r, q])
            new_line = line_a[...] - primal_step * line_grad
            line_a[...] = new_line
            return new_line - primal_step * line_grad

        sq_d = forward(bar0, prev_bar, lambda: new_cap + cap_diff, flow, dual_step, False)
        return prev_new, new_cap, cap_diff * cap_diff, weight, sq_p, sq_d

    first_diff = cap_new - cap_old
    carry = (
        prev_new,
        cap_new,
        first_diff * first_diff,
        jnp.ones((1, LANES), F32),
        sq_p,
        sq_d,
    )
    carry = lax.fori_loop(1, ITERS, later, carry)
    cap_out[...] = pltpu.roll(carry[1], lax.rem(LANES - me_t * own_n, LANES), 1)

    for r in range(ITERS):
        pltpu.make_async_copy(tbuf.at[r], tbuf.at[r], send_t.at[r]).wait()
    pltpu.make_async_copy(
        gat0.at[pl.ds(0, nr - 1)], gat0.at[pl.ds(0, nr - 1)], send_g.at[0]
    ).wait()
    for r in range(ITERS - 1):
        pltpu.make_async_copy(sbuf.at[r], sbuf.at[r], send_r.at[r]).wait()
        pltpu.make_async_copy(rbuf.at[r], rbuf.at[r], send_p.at[r]).wait()
        pltpu.make_async_copy(
            gat.at[r, pl.ds(0, nr - 1)], gat.at[r, pl.ds(0, nr - 1)], send_g.at[r + 1]
        ).wait()
    for n in range(1 + 2 * (ITERS - 1)):
        pltpu.make_async_copy(nb_src.at[n], nb_src.at[n], send_n.at[n]).wait()


def by_hour(x, y, cap, own):
    cb, hours, _, bs = x.shape

    def place(x_ref, y_ref, cap_ref, x_out, y_out, cap_out, sem):
        copies = []
        for c in range(cb):
            at = pl.ds(c * bs, bs)
            copies.append(pltpu.make_async_copy(x_ref.at[c], x_out.at[:, :, at], sem.at[0, c]))
            copies.append(pltpu.make_async_copy(y_ref.at[c], y_out.at[:, :, at], sem.at[1, c]))
        for copy in copies:
            copy.start()
        cap_out[...] = cap_ref[:, 0:own]
        for copy in copies:
            copy.wait()

    vmem = pl.BlockSpec(memory_space=pltpu.VMEM)
    hbm = pl.BlockSpec(memory_space=pl.ANY)
    shape = jax.ShapeDtypeStruct((hours, 1, cb * bs), F32)
    return pl.pallas_call(
        place,
        in_specs=[vmem, vmem, vmem],
        out_specs=(hbm, hbm, vmem),
        out_shape=(shape, shape, jax.ShapeDtypeStruct((1, own), F32)),
        scratch_shapes=[pltpu.SemaphoreType.DMA((2, cb))],
        compiler_params=pltpu.CompilerParams(vmem_limit_bytes=8 * 2**20),
    )(x, y, cap)


def in_hbm(value):
    return pltpu.with_memory_space_constraint(value, pltpu.HBM)


def body(
    start_primal,
    demand,
    unit_cost,
    build_cost,
    start_capacity,
    net_weights,
    net_columns,
    line_weights,
    line_source,
    generator_map,
):
    hours, _, width = start_primal.shape
    bs = net_weights.shape[3]
    cb = width // bs
    s_count = net_weights.shape[2]
    nl = line_weights.shape[1]
    nt = lax.axis_size("tm")
    nr = lax.axis_size("region")
    pairs = cb * s_count
    sizes = (hours, cb, bs, s_count, nl, nt, nr)
    vmem = pl.BlockSpec(memory_space=pltpu.VMEM)
    hbm = pl.BlockSpec(memory_space=pltpu.HBM)
    rounds = ITERS - 1
    dma = pltpu.SemaphoreType.DMA
    x_new, y_new, cap = pl.pallas_call(
        functools.partial(kernel, sizes),
        out_shape=(
            jax.ShapeDtypeStruct((cb, hours, bs), F32),
            jax.ShapeDtypeStruct((cb, hours, bs), F32),
            jax.ShapeDtypeStruct((1, LANES), F32),
        ),
        in_specs=[hbm] * 10,
        out_specs=(vmem, vmem, vmem),
        scratch_shapes=[
            pltpu.SMEM((s_count, 1, cb), jnp.int32),
            pltpu.SMEM(line_source.shape[::-1], jnp.int32),
            pltpu.SMEM(start_capacity.shape, F32),
            pltpu.SMEM(build_cost.shape, F32),
            pltpu.VMEM(generator_map.shape, jnp.int32),
            pltpu.VMEM((cb, 1, bs), F32),
            pltpu.VMEM((hours * cb, bs), F32),
            pltpu.VMEM((hours * cb, bs), F32),
            pltpu.VMEM((cb, s_count, bs, bs), F32),
            pltpu.VMEM((nl * bs, bs), F32),
            pltpu.VMEM((nl * bs, bs), BF16),
            pltpu.VMEM((nl * bs, bs), BF16),
            pltpu.VMEM((pairs, bs, bs), BF16),
            pltpu.VMEM((pairs, bs, bs), BF16),
            pltpu.VMEM((cb, hours, bs), F32),
            pltpu.VMEM((cb, hours, bs), F32),
            pltpu.VMEM((cb, 2 * hours, bs), BF16),
            pltpu.VMEM((cb, 2 * hours, bs), BF16),
            pltpu.VMEM((pairs, hours, bs), F32),
            pltpu.VMEM((3, hours, bs), F32),
            pltpu.VMEM((8, LANES), jnp.int32),
            pltpu.SMEM((8, LANES), jnp.int32),
            pltpu.VMEM((1, LANES), jnp.int32),
            pltpu.SMEM((1, LANES), jnp.int32),
            pltpu.VMEM((hours, bs), F32),
            pltpu.VMEM((8, bs), F32),
            pltpu.VMEM((hours + 8, bs), F32),
            pltpu.VMEM((nr, hours + 8, bs), F32),
            pltpu.VMEM((rounds, nr, hours, bs), F32),
            pltpu.VMEM((rounds, nr, hours, bs), F32),
            pltpu.VMEM((rounds, nr - 1, hours, bs), F32),
            pltpu.VMEM((ITERS, 1, 2 * LANES), F32),
            pltpu.VMEM((ITERS, nt - 1, 1, 2 * LANES), F32),
            pltpu.VMEM((rounds, 1, LANES), F32),
            pltpu.VMEM((rounds, nr - 1, 1, LANES), F32),
            pltpu.VMEM((1 + 2 * rounds, 1, LANES), F32),
            pltpu.VMEM((1 + 2 * rounds, 1, LANES), F32),
            dma((11,)),
            dma((cb,)),
            dma((ITERS,)),
            dma((ITERS,)),
            dma((rounds,)),
            dma((rounds,)),
            dma((ITERS,)),
            dma((ITERS,)),
            dma((rounds,)),
            dma((rounds,)),
            dma((1 + 2 * rounds,)),
            dma((1 + 2 * rounds,)),
        ],
        compiler_params=pltpu.CompilerParams(
            collective_id=0, has_side_effects=True, vmem_limit_bytes=40 * 2**20
        ),
    )(*(in_hbm(v) for v in (
        jnp.transpose(net_columns, (2, 0, 1)),
        jnp.transpose(line_source),
        start_capacity,
        build_cost,
        generator_map,
        unit_cost.reshape(cb, 1, bs),
        start_primal.reshape(hours * cb, bs),
        demand.reshape(hours * cb, bs),
        net_weights[0],
        line_weights.reshape(nl * bs, bs),
    )))
    parts = (cb, hours, 1, bs)
    return by_hour(x_new.reshape(parts), y_new.reshape(parts), cap, start_capacity.shape[1])


def solution(mesh):
    in_specs = (
        P("tm", "region", None),
        P("tm", "region", None),
        P("region", None),
        P("region", "tm"),
        P("region", "tm"),
        P("region", None, None, None, None),
        P("region", None, None),
        P("region", None, None, None),
        P(),
        P("region", None),
    )
    out_specs = (P("tm", "region", None), P("tm", "region", None), P("region", "tm"))
    return jax.shard_map(body, mesh=mesh, in_specs=in_specs, out_specs=out_specs, check_vma=False)
```

```python
import functools
import math

import jax
import jax.numpy as jnp
from jax import lax
from jax.experimental import pallas as pl
from jax.experimental.pallas import tpu as pltpu
from jax.sharding import PartitionSpec as P

ITERS = 4
STEP_SCALE = 0.2
EPSILON = 1e-06
HIGHEST = lax.Precision.HIGHEST
MESH = pl.DeviceIdType.MESH
F32 = jnp.float32
BF16 = jnp.bfloat16
LOW = float(jnp.finfo(jnp.float32).min)
LANES = 128


def split(value):
    high = value.astype(BF16)
    low = (value - high.astype(F32)).astype(BF16)
    return jnp.concatenate([high, low], axis=0)


def unrolled(first, last, by, step, carry):
    assert (last - first) % by == 0

    def some(n, c):
        for k in range(by):
            c = step(first + n * by + k, c)
        return c

    return lax.fori_loop(0, (last - first) // by, some, carry)


def dot_nt(a, b, precision=None):
    return lax.dot_general(
        a, b, (((1,), (1,)), ((), ())), precision=precision, preferred_element_type=F32
    )


def kernel(
    sizes,
    cols_hbm,
    src_hbm,
    cap_hbm,
    build_hbm,
    gm_hbm,
    unit_hbm,
    x_hbm,
    dem_hbm,
    w_hbm,
    lw_hbm,
    xs,
    ys,
    cap_out,
    cols_s,
    src_s,
    cap_s,
    build_s,
    gm_v,
    unit_v,
    xst,
    dst,
    wst,
    lw,
    lwh,
    lwl,
    wh,
    wl,
    tgt,
    grad,
    xb,
    yb,
    seg,
    extra,
    table_v,
    table_s,
    rank_v,
    rank_s,
    line_a,
    line_u,
    vx,
    gat0,
    gat,
    pbuf,
    rbuf,
    mt,
    tbuf,
    mr,
    sbuf,
    nb_src,
    nb_dst,
    load_sem,
    w_sem,
    send_t,
    recv_t,
    send_r,
    recv_r,
    send_g,
    recv_g,
    send_p,
    recv_p,
    send_n,
    recv_n,
):
    (hours, cb, bs, s_count, nl, nt, nr) = sizes
    pairs = cb * s_count
    me_t = lax.axis_index("tm")
    me_r = lax.axis_index("region")
    primal_count = hours * nt * nr * cb * bs + nr * LANES
    dual_count = hours * nt * nr * cb * bs
    couple = 1.0 / math.sqrt(hours * nt)

    cx = pltpu.make_async_copy(x_hbm, xst, load_sem.at[0])
    cu = pltpu.make_async_copy(unit_hbm, unit_v, load_sem.at[5])
    cc = pltpu.make_async_copy(cap_hbm, cap_s, load_sem.at[6])
    cbuild = pltpu.make_async_copy(build_hbm, build_s, load_sem.at[7])
    ck = pltpu.make_async_copy(cols_hbm, cols_s, load_sem.at[8])
    cs = pltpu.make_async_copy(src_hbm, src_s, load_sem.at[9])
    cg = pltpu.make_async_copy(gm_hbm, gm_v, load_sem.at[10])
    cd = pltpu.make_async_copy(dem_hbm, dst, load_sem.at[1])
    cl = pltpu.make_async_copy(lw_hbm, lw, load_sem.at[2])
    for c in (cx, cu, cc, cbuild):
        c.start()

    def rows_of(c):
        return pl.ds(c, hours, stride=cb)

    barrier = pltpu.get_barrier_semaphore()

    def offset_of(step, count):
        k = step + count // 2
        return jnp.where(k >= count, k - (count - 1), k)

    def around(me, k, count):
        at = me + k
        return jnp.where(at >= count, at - count, at)

    nx = 4 if nt % 4 == 0 else 1
    nz = nt // nx
    me_z, me_x = me_t // nx, me_t % nx

    def tm_partners(act):
        order = [(dz, dx) for dz in range(nz) for dx in range(nx) if dz or dx]
        order.sort(key=lambda d: -min(d[0], nz - d[0]) - min(d[1], nx - d[1]))
        for dz, dx in order:
            act(dz * nx + dx - 1, around(me_z, dz, nz) * nx + around(me_x, dx, nx))

    tm_partners(
        lambda slot, at: pl.semaphore_signal(
            barrier, inc=1, device_id=(at, me_r), device_id_type=MESH
        )
    )

    @pl.loop(0, nr - 1)
    def _(step):
        k = offset_of(step, nr)
        pl.semaphore_signal(
            barrier, inc=1, device_id=(me_t, around(me_r, k, nr)), device_id_type=MESH
        )

    for c in (ck, cs, cg, cd, cl):
        c.start()
    chunk = 5 if cb % 5 == 0 else 1
    w_copies = []
    for n in range(cb // chunk):
        at = pl.ds(n * chunk, chunk)
        w_copies.append(pltpu.make_async_copy(w_hbm.at[at], wst.at[at], w_sem.at[n]))
    for c in w_copies:
        c.start()

    lane = lax.broadcasted_iota(jnp.int32, (1, LANES), 1)

    own_n = LANES // nt
    cc.wait()
    cbuild.wait()
    cap_vec = jnp.zeros((1, LANES), F32)
    build_vec = jnp.zeros((1, LANES), F32)
    for k in range(own_n):
        here = lane == me_t * own_n + k
        cap_vec = jnp.where(here, cap_s[0, k], cap_vec)
        build_vec = jnp.where(here, build_s[0, k], build_vec)
    mt[0, :, 0:LANES] = cap_vec
    mt[0, :, LANES : 2 * LANES] = build_vec

    cx.wait()
    cu.wait()
    vx[0:hours, :] = xst[pl.ds(3, hours, stride=cb), :]
    vx[hours : hours + 8, :] = jnp.broadcast_to(unit_v[3], (8, LANES))
    nb_src[0] = xst[pl.ds((hours - 1) * cb, 1), :]

    pl.semaphore_wait(barrier, nt - 1 + nr - 1)

    def tm_send(r):
        def send(slot, at):
            pltpu.make_async_remote_copy(
                src_ref=mt.at[r],
                dst_ref=tbuf.at[r, slot],
                send_sem=send_t.at[r],
                recv_sem=recv_t.at[r],
                device_id=(at, me_r),
                device_id_type=MESH,
            ).start()

        tm_partners(send)

    def tm_sum(r):
        pltpu.make_async_copy(tbuf.at[r], tbuf.at[r], recv_t.at[r]).wait()
        parts = [mt[r]] + [tbuf[r, k] for k in range(nt - 1)]
        while len(parts) > 1:
            parts = [sum(parts[n + 1 : n + 2], parts[n]) for n in range(0, len(parts), 2)]
        return parts[0]

    def region_send(src, dst_of, send_sem, recv_sem):
        @pl.loop(0, nr - 1)
        def _(step):
            k = offset_of(step, nr)
            pltpu.make_async_remote_copy(
                src_ref=src(k),
                dst_ref=dst_of(k),
                send_sem=send_sem,
                recv_sem=recv_sem,
                device_id=(me_t, around(me_r, k, nr)),
                device_id_type=MESH,
            ).start()

    def to_next(n, r, by):
        pltpu.make_async_remote_copy(
            src_ref=nb_src.at[n],
            dst_ref=nb_dst.at[n],
            send_sem=send_n.at[n],
            recv_sem=recv_n.at[n],
            device_id=(around(me_t, (by + nt) % nt, nt), me_r),
            device_id_type=MESH,
        ).start()

    def next_wait(n):
        pltpu.make_async_copy(nb_dst.at[n], nb_dst.at[n], recv_n.at[n]).wait()

    tm_send(0)
    region_send(
        lambda k: vx, lambda k: gat0.at[me_r], send_g.at[0], recv_g.at[0]
    )
    to_next(0, 0, 1)
    gat0[me_r] = vx[...]

    ck.wait()
    cs.wait()
    cg.wait()


    def column(p):
        return cols_s[p % s_count, 0, p // s_count]

    col_vec = jnp.full((1, LANES), cb, jnp.int32)
    for p in range(pairs):
        col_vec = jnp.where(lane == p, column(p), col_vec)
    rank = jnp.zeros((1, LANES), jnp.int32)
    end_vec = jnp.zeros((1, LANES), jnp.int32)
    for q in range(pairs):
        c = column(q)
        ahead = (col_vec > c) | ((col_vec == c) & (lane > q))
        rank = rank + jnp.where(ahead, 1, 0)
        end_vec = end_vec + jnp.where(lane >= c, 1, 0)
    start_vec = jnp.where(lane == 0, 0, pltpu.roll(end_vec, 1, 1))
    rank_v[...] = rank
    c1 = pltpu.make_async_copy(rank_v, rank_s, load_sem.at[3])
    c1.start()

    sel_t = jnp.where(
        gm_v[...] == lax.broadcasted_iota(jnp.int32, (LANES, LANES), 0), 1.0, 0.0
    ).astype(F32)

    c1.wait()
    order = jnp.zeros((1, LANES), jnp.int32)
    order_row = jnp.zeros((1, LANES), jnp.int32)
    order_col = jnp.full((1, LANES), -1, jnp.int32)
    for p in range(pairs):
        here = lane == rank_s[0, p]
        order = jnp.where(here, p, order)
        order_row = jnp.where(here, p // s_count, order_row)
        order_col = jnp.where(here, column(p), order_col)
    goes_on = (order_col == pltpu.roll(order_col, 1, 1)) & (lane > 0)
    table_v[0:1, :] = order
    table_v[1:2, :] = order_row
    table_v[2:3, :] = jnp.where(goes_on, 1, 0)
    table_v[3:4, :] = jnp.maximum(end_vec - 1, 0)
    table_v[4:5, :] = jnp.where(end_vec > start_vec, 1, 0)
    table_v[5:8, :] = jnp.zeros((3, LANES), jnp.int32)
    c2 = pltpu.make_async_copy(table_v, table_s, load_sem.at[4])
    c2.start()

    for n, copy in enumerate(w_copies):
        copy.wait()

        @pl.loop(n * chunk, (n + 1) * chunk)
        def _(i):
            for s in range(s_count):
                w = wst[i, s]
                high = w.astype(BF16)
                wh[i * s_count + s] = high
                wl[i * s_count + s] = (w - high.astype(F32)).astype(BF16)

    cd.wait()
    cl.wait()

    def place_target(i, _):
        tgt[i] = dst[pl.ds(i, hours, stride=cb), :]
        return 0

    unrolled(0, cb, 5, place_target, 0)
    line_high = lw[...].astype(BF16)
    lwh[...] = line_high
    lwl[...] = (lw[...] - line_high.astype(F32)).astype(BF16)

    def primal_block(c, x, g, step):
        low = jnp.where(c == 3, LOW, 0.0)
        new = jnp.maximum(x - step * g, low)
        change = new - x
        bar = new + change
        xs[rows_of(c), :] = new
        xb[c] = split(bar)
        return bar, change * change

    def fold(sq):
        return jnp.sum(sq.reshape(hours // 8, 8, LANES), axis=0)

    first_step = STEP_SCALE

    def first_primal(c, acc):
        x = xst[pl.ds(c, hours, stride=cb), :]
        g = jnp.broadcast_to(unit_v[c], (hours, LANES))
        bar, sq = primal_block(c, x, g, first_step)
        return bar, acc + fold(sq)

    zero8 = jnp.zeros((8, LANES), F32)
    bar0, sq_p = first_primal(0, zero8)
    sq_p = unrolled(1, cb, 4, lambda c, a: first_primal(c, a)[1], sq_p)

    def network(i):
        x3 = jnp.concatenate([xb[cols_s[s, 0, i]] for s in range(s_count)], axis=1)
        high = jnp.concatenate([wh[i * s_count + s] for s in range(s_count)], axis=0)
        low = jnp.concatenate([wl[i * s_count + s] for s in range(s_count)], axis=0)
        both = jnp.dot(x3, high, preferred_element_type=F32)
        last = jnp.dot(x3[0:hours], low, preferred_element_type=F32)
        return both[0:hours] + both[hours:] + last

    def dual_block(i, rest, step, first):
        low = jnp.where(i < 3, LOW, 0.0)
        move = step * rest
        if first:
            new = jnp.maximum(move, low)
            change = new
        else:
            old = ys[rows_of(i), :]
            new = jnp.maximum(old + move, low)
            change = new - old
        ys[rows_of(i), :] = new
        yb[i] = split(new)
        return fold(change * change)

    def target_of(i):
        return dst[pl.ds(i, hours, stride=cb), :]

    def line_apply(block_of):
        parts = jnp.concatenate([block_of(src_s[j, me_r]) for j in range(nl)], axis=1)
        high = parts.astype(BF16)
        low = (parts - high.astype(F32)).astype(BF16)
        return (
            jnp.dot(high, lwh[...], preferred_element_type=F32)
            + jnp.dot(low, lwh[...], preferred_element_type=F32)
            + jnp.dot(high, lwl[...], preferred_element_type=F32)
        )

    row = lax.broadcasted_iota(jnp.int32, (hours, LANES), 0)
    has_before = jnp.where(me_t > 0, 1.0, 0.0).astype(F32)
    has_after = jnp.where(me_t < nt - 1, 1.0, 0.0).astype(F32)

    def forward(bar0, prev_bar, cap_bar, line_flow, step, first):
        earlier = pltpu.roll(bar0, 1, 0)
        earlier = jnp.where(row == 0, prev_bar * has_before, earlier)

        def capacity_term():
            return couple * jnp.dot(
                jnp.broadcast_to(cap_bar(), (8, LANES)),
                sel_t,
                precision=HIGHEST,
                preferred_element_type=F32,
            )[0:1]

        def plain(i, a):
            return a + dual_block(i, tgt[i] - network(i), step, first)

        if first:
            sq = unrolled(3, cb, 11, plain, zero8)
        else:
            picked = capacity_term()
            sq = zero8
            for i in range(3, cb):
                sq = plain(i, sq)
        sq = sq + dual_block(0, tgt[0] + earlier - network(0), step, first)
        rest = tgt[2] - network(2)
        last = tgt[1] - network(1)
        if first:
            picked = capacity_term()
        sq = sq + dual_block(2, rest - picked, step, first)
        return sq + dual_block(1, last - line_flow(), step, first)

    lane_low = lane < LANES // 2

    def pack(p, d):
        p = jnp.sum(p, axis=0, keepdims=True)
        d = jnp.sum(d, axis=0, keepdims=True)
        p = p + pltpu.roll(p, LANES // 2, 1)
        d = d + pltpu.roll(d, LANES // 2, 1)
        return jnp.where(lane_low, p, d)

    gathered = []

    def first_capacity():
        total = tm_sum(0)
        cap = total[:, 0:LANES]
        build = total[:, LANES : 2 * LANES]
        new_cap = jnp.maximum(cap - first_step * build, 0.0)
        gathered.extend([cap, build, new_cap])
        return new_cap + (new_cap - cap)

    def first_flow():
        pltpu.make_async_copy(
            gat0.at[pl.ds(0, nr - 1)], gat0.at[pl.ds(0, nr - 1)], recv_g.at[0]
        ).wait()
        both = line_apply(lambda q: gat0[q])
        line_unit = both[hours : hours + 1]
        line_x = both[0:hours]
        line_u[...] = jnp.broadcast_to(line_unit, (8, LANES))
        new_line = line_x - first_step * line_unit
        line_a[...] = new_line
        return new_line - first_step * line_unit

    next_wait(0)
    prev_old = nb_dst[0]
    prev_new = jnp.maximum(prev_old - first_step * unit_v[0], 0.0)
    prev_bar = prev_new + (prev_new - prev_old)
    sq_d = forward(bar0, prev_bar, first_capacity, first_flow, first_step, True)
    cap_old, build, cap_new = gathered

    c2.wait()

    def later(it, carry):
        prev_x, cap, cap_change, weight, sq_p, sq_d = carry
        r = it - 1
        mt[it, :, 0:LANES] = jnp.sum(ys[rows_of(2), :], axis=0, keepdims=True)
        mt[it, :, LANES : 2 * LANES] = pack(sq_p, sq_d)
        nb_src[1 + r] = ys[0:1, :]
        tm_send(it)
        to_next(1 + r, r, -1)

        y1 = yb[1]
        terms = (
            dot_nt(y1[0:hours], lwh[...])
            + dot_nt(y1[hours:], lwh[...])
            + dot_nt(y1[0:hours], lwl[...])
        )
        for k in range(nr):
            q = around(me_r, k, nr)
            total = jnp.zeros((hours, LANES), F32)
            for j in range(nl):
                on = jnp.where(src_s[j, me_r] == q, 1.0, 0.0).astype(F32)
                total = total + on * terms[:, j * bs : (j + 1) * bs]
            pbuf[r, k] = total
        region_send(
            lambda k: pbuf.at[r, k], lambda k: rbuf.at[r, k - 1], send_p.at[r], recv_p.at[r]
        )

        def pair(n, total):
            p = table_s[0, n]
            y = yb[table_s[1, n]]
            keep = table_s[2, n].astype(F32)
            both = dot_nt(y, wh[p])
            low = dot_nt(y[0:hours], wl[p])
            total = keep * total + (both[0:hours] + both[hours:] + low)
            seg[n] = total
            return total

        unrolled(0, pairs, 15, pair, jnp.zeros((hours, LANES), F32))

        def gradient(c, _):
            grad[c] = unit_v[c] - table_s[4, c].astype(F32) * seg[table_s[3, c]]
            return 0

        unrolled(0, cb, 5, gradient, 0)
        nb_src[4 + r] = grad[0, hours - 1 : hours, :]
        to_next(4 + r, r, 1)

        next_wait(1 + r)
        following = pltpu.roll(ys[rows_of(0), :], hours - 1, 0)
        following = jnp.where(row == hours - 1, nb_dst[1 + r] * has_after, following)
        grad[0] = grad[0] + following

        total = tm_sum(it)
        col_sums = total[:, 0:LANES]
        region_sums = total[:, LANES : 2 * LANES] + pack(
            cap_change, jnp.zeros_like(cap_change)
        )
        mr[r] = region_sums
        region_send(
            lambda k: mr.at[r], lambda k: sbuf.at[r, k - 1], send_r.at[r], recv_r.at[r]
        )
        capacity_grad = couple * dot_nt(
            jnp.broadcast_to(col_sums, (8, LANES)), sel_t, precision=HIGHEST
        )[0:1]

        pltpu.make_async_copy(rbuf.at[r], rbuf.at[r], recv_p.at[r]).wait()
        line_back = pbuf[r, 0]
        for k in range(nr - 1):
            line_back = line_back + rbuf[r, k]
        flow_grad = grad[3] - line_back
        grad[3] = flow_grad
        gat[r, me_r] = flow_grad
        region_send(
            lambda k: gat.at[r, me_r],
            lambda k: gat.at[r, me_r],
            send_g.at[it],
            recv_g.at[it],
        )
        next_wait(4 + r)
        prev_grad = nb_dst[4 + r] + ys[0:1, :]

        pltpu.make_async_copy(sbuf.at[r], sbuf.at[r], recv_r.at[r]).wait()
        sums = mr[r]
        for k in range(nr - 1):
            sums = sums + sbuf[r, k]
        total_p = jnp.sum(jnp.where(lane_low, sums, 0.0), axis=1, keepdims=True)
        total_d = jnp.sum(jnp.where(lane_low, 0.0, sums), axis=1, keepdims=True)
        total_p = jnp.broadcast_to(total_p, (1, LANES))
        total_d = jnp.broadcast_to(total_d, (1, LANES))
        weight = jnp.sqrt(
            weight
            * jnp.sqrt(total_p / primal_count + EPSILON)
            / jnp.sqrt(total_d / dual_count + EPSILON)
        )
        primal_step = STEP_SCALE / weight
        dual_step = STEP_SCALE * weight

        def primal(c, a):
            bar, sq = primal_block(c, xs[rows_of(c), :], grad[c], primal_step)
            return bar, a + fold(sq)

        bar0, sq_p = primal(0, zero8)
        sq_p = unrolled(1, cb, 6, lambda c, a: primal(c, a)[1], sq_p)
        new_cap = jnp.maximum(cap - primal_step * (build - capacity_grad), 0.0)
        cap_diff = new_cap - cap
        prev_new = jnp.maximum(prev_x - primal_step * prev_grad, 0.0)
        prev_bar = prev_new + (prev_new - prev_x)

        def flow():
            pltpu.make_async_copy(
                gat.at[r, pl.ds(0, nr - 1)], gat.at[r, pl.ds(0, nr - 1)], recv_g.at[it]
            ).wait()
            line_grad = line_apply(lambda q: gat[r, q])
            new_line = line_a[...] - primal_step * line_grad
            line_a[...] = new_line
            return new_line - primal_step * line_grad

        sq_d = forward(bar0, prev_bar, lambda: new_cap + cap_diff, flow, dual_step, False)
        return prev_new, new_cap, cap_diff * cap_diff, weight, sq_p, sq_d

    first_diff = cap_new - cap_old
    carry = (
        prev_new,
        cap_new,
        first_diff * first_diff,
        jnp.ones((1, LANES), F32),
        sq_p,
        sq_d,
    )
    carry = lax.fori_loop(1, ITERS, later, carry)
    cap_out[...] = pltpu.roll(carry[1], lax.rem(LANES - me_t * own_n, LANES), 1)

    for r in range(ITERS):
        pltpu.make_async_copy(tbuf.at[r], tbuf.at[r], send_t.at[r]).wait()
    pltpu.make_async_copy(
        gat0.at[pl.ds(0, nr - 1)], gat0.at[pl.ds(0, nr - 1)], send_g.at[0]
    ).wait()
    for r in range(ITERS - 1):
        pltpu.make_async_copy(sbuf.at[r], sbuf.at[r], send_r.at[r]).wait()
        pltpu.make_async_copy(rbuf.at[r], rbuf.at[r], send_p.at[r]).wait()
        pltpu.make_async_copy(
            gat.at[r, pl.ds(0, nr - 1)], gat.at[r, pl.ds(0, nr - 1)], send_g.at[r + 1]
        ).wait()
    for n in range(1 + 2 * (ITERS - 1)):
        pltpu.make_async_copy(nb_src.at[n], nb_src.at[n], send_n.at[n]).wait()


def to_results(x, y, cap, own):
    rows = x.shape[0]
    pieces = 4

    def place(x_ref, y_ref, cap_ref, x_out, y_out, cap_out, sem):
        copies = []
        for n in range(pieces):
            at = pl.ds(n * (rows // pieces), rows // pieces)
            copies.append(pltpu.make_async_copy(x_ref.at[at], x_out.at[at], sem.at[0, n]))
            copies.append(pltpu.make_async_copy(y_ref.at[at], y_out.at[at], sem.at[1, n]))
        for copy in copies:
            copy.start()
        cap_out[...] = cap_ref[:, 0:own]
        for copy in copies:
            copy.wait()

    vmem = pl.BlockSpec(memory_space=pltpu.VMEM)
    hbm = pl.BlockSpec(memory_space=pl.ANY)
    shape = jax.ShapeDtypeStruct(x.shape, F32)
    return pl.pallas_call(
        place,
        in_specs=[vmem, vmem, vmem],
        out_specs=(hbm, hbm, vmem),
        out_shape=(shape, shape, jax.ShapeDtypeStruct((1, own), F32)),
        scratch_shapes=[pltpu.SemaphoreType.DMA((2, pieces))],
        compiler_params=pltpu.CompilerParams(vmem_limit_bytes=8 * 2**20),
    )(x, y, cap)


def in_hbm(value):
    return pltpu.with_memory_space_constraint(value, pltpu.HBM)


def body(
    start_primal,
    demand,
    unit_cost,
    build_cost,
    start_capacity,
    net_weights,
    net_columns,
    line_weights,
    line_source,
    generator_map,
):
    hours, _, width = start_primal.shape
    bs = net_weights.shape[3]
    cb = width // bs
    s_count = net_weights.shape[2]
    nl = line_weights.shape[1]
    nt = lax.axis_size("tm")
    nr = lax.axis_size("region")
    pairs = cb * s_count
    sizes = (hours, cb, bs, s_count, nl, nt, nr)
    vmem = pl.BlockSpec(memory_space=pltpu.VMEM)
    hbm = pl.BlockSpec(memory_space=pltpu.HBM)
    rounds = ITERS - 1
    dma = pltpu.SemaphoreType.DMA
    x_new, y_new, cap = pl.pallas_call(
        functools.partial(kernel, sizes),
        out_shape=(
            jax.ShapeDtypeStruct((hours * cb, bs), F32),
            jax.ShapeDtypeStruct((hours * cb, bs), F32),
            jax.ShapeDtypeStruct((1, LANES), F32),
        ),
        in_specs=[hbm] * 10,
        out_specs=(vmem, vmem, vmem),
        scratch_shapes=[
            pltpu.SMEM((s_count, 1, cb), jnp.int32),
            pltpu.SMEM(line_source.shape[::-1], jnp.int32),
            pltpu.SMEM(start_capacity.shape, F32),
            pltpu.SMEM(build_cost.shape, F32),
            pltpu.VMEM(generator_map.shape, jnp.int32),
            pltpu.VMEM((cb, 1, bs), F32),
            pltpu.VMEM((hours * cb, bs), F32),
            pltpu.VMEM((hours * cb, bs), F32),
            pltpu.VMEM((cb, s_count, bs, bs), F32),
            pltpu.VMEM((nl * bs, bs), F32),
            pltpu.VMEM((nl * bs, bs), BF16),
            pltpu.VMEM((nl * bs, bs), BF16),
            pltpu.VMEM((pairs, bs, bs), BF16),
            pltpu.VMEM((pairs, bs, bs), BF16),
            pltpu.VMEM((cb, hours, bs), F32),
            pltpu.VMEM((cb, hours, bs), F32),
            pltpu.VMEM((cb, 2 * hours, bs), BF16),
            pltpu.VMEM((cb, 2 * hours, bs), BF16),
            pltpu.VMEM((pairs, hours, bs), F32),
            pltpu.VMEM((3, hours, bs), F32),
            pltpu.VMEM((8, LANES), jnp.int32),
            pltpu.SMEM((8, LANES), jnp.int32),
            pltpu.VMEM((1, LANES), jnp.int32),
            pltpu.SMEM((1, LANES), jnp.int32),
            pltpu.VMEM((hours, bs), F32),
            pltpu.VMEM((8, bs), F32),
            pltpu.VMEM((hours + 8, bs), F32),
            pltpu.VMEM((nr, hours + 8, bs), F32),
            pltpu.VMEM((rounds, nr, hours, bs), F32),
            pltpu.VMEM((rounds, nr, hours, bs), F32),
            pltpu.VMEM((rounds, nr - 1, hours, bs), F32),
            pltpu.VMEM((ITERS, 1, 2 * LANES), F32),
            pltpu.VMEM((ITERS, nt - 1, 1, 2 * LANES), F32),
            pltpu.VMEM((rounds, 1, LANES), F32),
            pltpu.VMEM((rounds, nr - 1, 1, LANES), F32),
            pltpu.VMEM((1 + 2 * rounds, 1, LANES), F32),
            pltpu.VMEM((1 + 2 * rounds, 1, LANES), F32),
            dma((11,)),
            dma((cb // 5 if cb % 5 == 0 else cb,)),
            dma((ITERS,)),
            dma((ITERS,)),
            dma((rounds,)),
            dma((rounds,)),
            dma((ITERS,)),
            dma((ITERS,)),
            dma((rounds,)),
            dma((rounds,)),
            dma((1 + 2 * rounds,)),
            dma((1 + 2 * rounds,)),
        ],
        compiler_params=pltpu.CompilerParams(
            collective_id=0, has_side_effects=True, vmem_limit_bytes=40 * 2**20
        ),
    )(*(in_hbm(v) for v in (
        jnp.transpose(net_columns, (2, 0, 1)),
        jnp.transpose(line_source),
        start_capacity,
        build_cost,
        generator_map,
        unit_cost.reshape(cb, 1, bs),
        start_primal.reshape(hours * cb, bs),
        demand.reshape(hours * cb, bs),
        net_weights[0],
        line_weights.reshape(nl * bs, bs),
    )))
    x_new, y_new, capacity = to_results(x_new, y_new, cap, start_capacity.shape[1])
    return x_new.reshape(hours, 1, width), y_new.reshape(hours, 1, width), capacity


def solution(mesh):
    in_specs = (
        P("tm", "region", None),
        P("tm", "region", None),
        P("region", None),
        P("region", "tm"),
        P("region", "tm"),
        P("region", None, None, None, None),
        P("region", None, None),
        P("region", None, None, None),
        P(),
        P("region", None),
    )
    out_specs = (P("tm", "region", None), P("tm", "region", None), P("region", "tm"))
    return jax.shard_map(body, mesh=mesh, in_specs=in_specs, out_specs=out_specs, check_vma=False)
```

```python
import functools
import math

import jax
import jax.numpy as jnp
from jax import lax
from jax.experimental import pallas as pl
from jax.experimental.pallas import tpu as pltpu
from jax.sharding import PartitionSpec as P

ITERS = 4
STEP_SCALE = 0.2
EPSILON = 1e-06
HIGHEST = lax.Precision.HIGHEST
MESH = pl.DeviceIdType.MESH
F32 = jnp.float32
BF16 = jnp.bfloat16
LOW = float(jnp.finfo(jnp.float32).min)
LANES = 128


def split(value):
    high = value.astype(BF16)
    low = (value - high.astype(F32)).astype(BF16)
    return jnp.concatenate([high, low], axis=0)


def unrolled(first, last, by, step, carry):
    assert (last - first) % by == 0

    def some(n, c):
        for k in range(by):
            c = step(first + n * by + k, c)
        return c

    return lax.fori_loop(0, (last - first) // by, some, carry)


def dot_nt(a, b, precision=None):
    return lax.dot_general(
        a, b, (((1,), (1,)), ((), ())), precision=precision, preferred_element_type=F32
    )


def kernel(
    sizes,
    cols_hbm,
    src_hbm,
    cap_hbm,
    build_hbm,
    gm_hbm,
    unit_hbm,
    x_hbm,
    dem_hbm,
    w_hbm,
    lw_hbm,
    xs,
    ys,
    cap_out,
    cols_s,
    src_s,
    cap_s,
    build_s,
    gm_v,
    unit_v,
    xst,
    dst,
    wst,
    lw,
    lwh,
    lwl,
    wh,
    wl,
    tgt,
    grad,
    xb,
    yb,
    seg,
    extra,
    table_v,
    table_s,
    rank_v,
    rank_s,
    line_a,
    line_u,
    vx,
    gat0,
    gat,
    pbuf,
    rbuf,
    mt,
    tbuf,
    mr,
    sbuf,
    nb_src,
    nb_dst,
    load_sem,
    w_sem,
    send_t,
    recv_t,
    send_r,
    recv_r,
    send_g,
    recv_g,
    send_p,
    recv_p,
    send_n,
    recv_n,
):
    (hours, cb, bs, s_count, nl, nt, nr) = sizes
    pairs = cb * s_count
    me_t = lax.axis_index("tm")
    me_r = lax.axis_index("region")
    primal_count = hours * nt * nr * cb * bs + nr * LANES
    dual_count = hours * nt * nr * cb * bs
    couple = 1.0 / math.sqrt(hours * nt)

    cx = pltpu.make_async_copy(x_hbm, xst, load_sem.at[0])
    cu = pltpu.make_async_copy(unit_hbm, unit_v, load_sem.at[5])
    cc = pltpu.make_async_copy(cap_hbm, cap_s, load_sem.at[6])
    cbuild = pltpu.make_async_copy(build_hbm, build_s, load_sem.at[7])
    ck = pltpu.make_async_copy(cols_hbm, cols_s, load_sem.at[8])
    cs = pltpu.make_async_copy(src_hbm, src_s, load_sem.at[9])
    cg = pltpu.make_async_copy(gm_hbm, gm_v, load_sem.at[10])
    cd = pltpu.make_async_copy(dem_hbm, dst, load_sem.at[1])
    cl = pltpu.make_async_copy(lw_hbm, lw, load_sem.at[2])
    for c in (cx, cu, cc, cbuild):
        c.start()

    def rows_of(c):
        return pl.ds(c, hours, stride=cb)

    barrier = pltpu.get_barrier_semaphore()

    def offset_of(step, count):
        k = step + count // 2
        return jnp.where(k >= count, k - (count - 1), k)

    def around(me, k, count):
        at = me + k
        return jnp.where(at >= count, at - count, at)

    nx = 4 if nt % 4 == 0 else 1
    nz = nt // nx
    me_z, me_x = me_t // nx, me_t % nx

    def tm_partners(act):
        order = [(dz, dx) for dz in range(nz) for dx in range(nx) if dz or dx]
        order.sort(key=lambda d: -min(d[0], nz - d[0]) - min(d[1], nx - d[1]))
        for dz, dx in order:
            act(dz * nx + dx - 1, around(me_z, dz, nz) * nx + around(me_x, dx, nx))

    tm_partners(
        lambda slot, at: pl.semaphore_signal(
            barrier, inc=1, device_id=(at, me_r), device_id_type=MESH
        )
    )

    @pl.loop(0, nr - 1)
    def _(step):
        k = offset_of(step, nr)
        pl.semaphore_signal(
            barrier, inc=1, device_id=(me_t, around(me_r, k, nr)), device_id_type=MESH
        )

    for c in (ck, cs, cg, cd, cl):
        c.start()
    chunk = 5 if cb % 5 == 0 else 1
    w_copies = []
    for n in range(cb // chunk):
        at = pl.ds(n * chunk, chunk)
        w_copies.append(pltpu.make_async_copy(w_hbm.at[at], wst.at[at], w_sem.at[n]))
    for c in w_copies:
        c.start()

    lane = lax.broadcasted_iota(jnp.int32, (1, LANES), 1)

    own_n = LANES // nt
    cc.wait()
    cbuild.wait()
    cap_vec = jnp.zeros((1, LANES), F32)
    build_vec = jnp.zeros((1, LANES), F32)
    for k in range(own_n):
        here = lane == me_t * own_n + k
        cap_vec = jnp.where(here, cap_s[0, k], cap_vec)
        build_vec = jnp.where(here, build_s[0, k], build_vec)
    mt[0, :, 0:LANES] = cap_vec
    mt[0, :, LANES : 2 * LANES] = build_vec

    cx.wait()
    cu.wait()
    vx[0:hours, :] = xst[pl.ds(3, hours, stride=cb), :]
    vx[hours : hours + 8, :] = jnp.broadcast_to(unit_v[3], (8, LANES))
    nb_src[0] = xst[pl.ds((hours - 1) * cb, 1), :]

    pl.semaphore_wait(barrier, nt - 1 + nr - 1)

    def tm_send(r):
        def send(slot, at):
            pltpu.make_async_remote_copy(
                src_ref=mt.at[r],
                dst_ref=tbuf.at[r, slot],
                send_sem=send_t.at[r],
                recv_sem=recv_t.at[r],
                device_id=(at, me_r),
                device_id_type=MESH,
            ).start()

        tm_partners(send)

    def tree(parts):
        while len(parts) > 1:
            parts = [sum(parts[n + 1 : n + 2], parts[n]) for n in range(0, len(parts), 2)]
        return parts[0]

    def tm_sum(r):
        pltpu.make_async_copy(tbuf.at[r], tbuf.at[r], recv_t.at[r]).wait()
        return tree([mt[r]] + [tbuf[r, k] for k in range(nt - 1)])

    def region_send(src, dst_of, send_sem, recv_sem):
        @pl.loop(0, nr - 1)
        def _(step):
            k = offset_of(step, nr)
            pltpu.make_async_remote_copy(
                src_ref=src(k),
                dst_ref=dst_of(k),
                send_sem=send_sem,
                recv_sem=recv_sem,
                device_id=(me_t, around(me_r, k, nr)),
                device_id_type=MESH,
            ).start()

    def to_next(n, r, by):
        pltpu.make_async_remote_copy(
            src_ref=nb_src.at[n],
            dst_ref=nb_dst.at[n],
            send_sem=send_n.at[n],
            recv_sem=recv_n.at[n],
            device_id=(around(me_t, (by + nt) % nt, nt), me_r),
            device_id_type=MESH,
        ).start()

    def next_wait(n):
        pltpu.make_async_copy(nb_dst.at[n], nb_dst.at[n], recv_n.at[n]).wait()

    tm_send(0)
    region_send(
        lambda k: vx, lambda k: gat0.at[me_r], send_g.at[0], recv_g.at[0]
    )
    to_next(0, 0, 1)
    gat0[me_r] = vx[...]

    ck.wait()
    cs.wait()
    cg.wait()


    def column(p):
        return cols_s[p % s_count, 0, p // s_count]

    col_vec = jnp.full((1, LANES), cb, jnp.int32)
    for p in range(pairs):
        col_vec = jnp.where(lane == p, column(p), col_vec)
    rank = jnp.zeros((1, LANES), jnp.int32)
    end_vec = jnp.zeros((1, LANES), jnp.int32)
    for q in range(pairs):
        c = column(q)
        ahead = (col_vec > c) | ((col_vec == c) & (lane > q))
        rank = rank + jnp.where(ahead, 1, 0)
        end_vec = end_vec + jnp.where(lane >= c, 1, 0)
    start_vec = jnp.where(lane == 0, 0, pltpu.roll(end_vec, 1, 1))
    rank_v[...] = rank
    c1 = pltpu.make_async_copy(rank_v, rank_s, load_sem.at[3])
    c1.start()

    sel_t = jnp.where(
        gm_v[...] == lax.broadcasted_iota(jnp.int32, (LANES, LANES), 0), 1.0, 0.0
    ).astype(F32)

    c1.wait()
    order = jnp.zeros((1, LANES), jnp.int32)
    order_row = jnp.zeros((1, LANES), jnp.int32)
    order_col = jnp.full((1, LANES), -1, jnp.int32)
    for p in range(pairs):
        here = lane == rank_s[0, p]
        order = jnp.where(here, p, order)
        order_row = jnp.where(here, p // s_count, order_row)
        order_col = jnp.where(here, column(p), order_col)
    goes_on = (order_col == pltpu.roll(order_col, 1, 1)) & (lane > 0)
    table_v[0:1, :] = order
    table_v[1:2, :] = order_row
    table_v[2:3, :] = jnp.where(goes_on, 1, 0)
    table_v[3:4, :] = jnp.maximum(end_vec - 1, 0)
    table_v[4:5, :] = jnp.where(end_vec > start_vec, 1, 0)
    table_v[5:8, :] = jnp.zeros((3, LANES), jnp.int32)
    c2 = pltpu.make_async_copy(table_v, table_s, load_sem.at[4])
    c2.start()

    for n, copy in enumerate(w_copies):
        copy.wait()

        @pl.loop(n * chunk, (n + 1) * chunk)
        def _(i):
            for s in range(s_count):
                w = wst[i, s]
                high = w.astype(BF16)
                wh[i * s_count + s] = high
                wl[i * s_count + s] = (w - high.astype(F32)).astype(BF16)

    cd.wait()
    cl.wait()

    def place_target(i, _):
        tgt[i] = dst[pl.ds(i, hours, stride=cb), :]
        return 0

    unrolled(0, cb, 5, place_target, 0)
    line_high = lw[...].astype(BF16)
    lwh[...] = line_high
    lwl[...] = (lw[...] - line_high.astype(F32)).astype(BF16)

    def primal_block(c, x, g, step):
        low = jnp.where(c == 3, LOW, 0.0)
        new = jnp.maximum(x - step * g, low)
        change = new - x
        bar = new + change
        xs[rows_of(c), :] = new
        xb[c] = split(bar)
        return bar, change * change

    def fold(sq):
        return jnp.sum(sq.reshape(hours // 8, 8, LANES), axis=0)

    first_step = STEP_SCALE

    def first_primal(c, acc):
        x = xst[pl.ds(c, hours, stride=cb), :]
        g = jnp.broadcast_to(unit_v[c], (hours, LANES))
        bar, sq = primal_block(c, x, g, first_step)
        return bar, acc + fold(sq)

    zero8 = jnp.zeros((8, LANES), F32)
    bar0, sq_p = first_primal(0, zero8)
    sq_p = unrolled(1, cb, 4, lambda c, a: first_primal(c, a)[1], sq_p)

    def network(i):
        x3 = jnp.concatenate([xb[cols_s[s, 0, i]] for s in range(s_count)], axis=1)
        high = jnp.concatenate([wh[i * s_count + s] for s in range(s_count)], axis=0)
        low = jnp.concatenate([wl[i * s_count + s] for s in range(s_count)], axis=0)
        both = jnp.dot(x3, high, preferred_element_type=F32)
        last = jnp.dot(x3[0:hours], low, preferred_element_type=F32)
        return both[0:hours] + both[hours:] + last

    def dual_block(i, rest, step, first):
        low = jnp.where(i < 3, LOW, 0.0)
        move = step * rest
        if first:
            new = jnp.maximum(move, low)
            change = new
        else:
            old = ys[rows_of(i), :]
            new = jnp.maximum(old + move, low)
            change = new - old
        ys[rows_of(i), :] = new
        yb[i] = split(new)
        return fold(change * change)

    def target_of(i):
        return dst[pl.ds(i, hours, stride=cb), :]

    def line_apply(block_of):
        parts = jnp.concatenate([block_of(src_s[j, me_r]) for j in range(nl)], axis=1)
        high = parts.astype(BF16)
        low = (parts - high.astype(F32)).astype(BF16)
        return (
            jnp.dot(high, lwh[...], preferred_element_type=F32)
            + jnp.dot(low, lwh[...], preferred_element_type=F32)
            + jnp.dot(high, lwl[...], preferred_element_type=F32)
        )

    row = lax.broadcasted_iota(jnp.int32, (hours, LANES), 0)
    has_before = jnp.where(me_t > 0, 1.0, 0.0).astype(F32)
    has_after = jnp.where(me_t < nt - 1, 1.0, 0.0).astype(F32)

    def forward(bar0, prev_bar, cap_bar, line_flow, step, first):
        earlier = pltpu.roll(bar0, 1, 0)
        earlier = jnp.where(row == 0, prev_bar * has_before, earlier)

        def capacity_term():
            return couple * jnp.dot(
                jnp.broadcast_to(cap_bar(), (8, LANES)),
                sel_t,
                precision=HIGHEST,
                preferred_element_type=F32,
            )[0:1]

        def plain(i, a):
            return a + dual_block(i, tgt[i] - network(i), step, first)

        if first:
            sq = unrolled(3, cb, 11, plain, zero8)
        else:
            picked = capacity_term()
            sq = zero8
            for i in range(3, cb):
                sq = plain(i, sq)
        sq = sq + dual_block(0, tgt[0] + earlier - network(0), step, first)
        rest = tgt[2] - network(2)
        last = tgt[1] - network(1)
        if first:
            picked = capacity_term()
        sq = sq + dual_block(2, rest - picked, step, first)
        cols = jnp.sum(ys[rows_of(2), :], axis=0, keepdims=True)
        return sq + dual_block(1, last - line_flow(), step, first), cols

    lane_low = lane < LANES // 2

    def halves(v):
        v = jnp.sum(v, axis=0, keepdims=True)
        return v + pltpu.roll(v, LANES // 2, 1)

    gathered = []

    def first_capacity():
        total = tm_sum(0)
        cap = total[:, 0:LANES]
        build = total[:, LANES : 2 * LANES]
        new_cap = jnp.maximum(cap - first_step * build, 0.0)
        gathered.extend([cap, build, new_cap])
        return new_cap + (new_cap - cap)

    def first_flow():
        pltpu.make_async_copy(
            gat0.at[pl.ds(0, nr - 1)], gat0.at[pl.ds(0, nr - 1)], recv_g.at[0]
        ).wait()
        both = line_apply(lambda q: gat0[q])
        line_unit = both[hours : hours + 1]
        line_x = both[0:hours]
        line_u[...] = jnp.broadcast_to(line_unit, (8, LANES))
        new_line = line_x - first_step * line_unit
        line_a[...] = new_line
        return new_line - first_step * line_unit

    next_wait(0)
    prev_old = nb_dst[0]
    prev_new = jnp.maximum(prev_old - first_step * unit_v[0], 0.0)
    prev_bar = prev_new + (prev_new - prev_old)
    sq_p = halves(sq_p)
    sq_d, col_own = forward(bar0, prev_bar, first_capacity, first_flow, first_step, True)
    cap_old, build, cap_new = gathered

    c2.wait()

    def later(it, carry):
        prev_x, cap, cap_change, weight, sq_p, sq_d, col_own = carry
        r = it - 1
        mt[it, :, 0:LANES] = col_own
        mt[it, :, LANES : 2 * LANES] = jnp.where(lane_low, sq_p, halves(sq_d))
        nb_src[1 + r] = ys[0:1, :]
        tm_send(it)
        to_next(1 + r, r, -1)

        y1 = yb[1]
        terms = (
            dot_nt(y1[0:hours], lwh[...])
            + dot_nt(y1[hours:], lwh[...])
            + dot_nt(y1[0:hours], lwl[...])
        )
        for k in range(nr):
            q = around(me_r, k, nr)
            total = jnp.zeros((hours, LANES), F32)
            for j in range(nl):
                on = jnp.where(src_s[j, me_r] == q, 1.0, 0.0).astype(F32)
                total = total + on * terms[:, j * bs : (j + 1) * bs]
            pbuf[r, k] = total
        region_send(
            lambda k: pbuf.at[r, k], lambda k: rbuf.at[r, k - 1], send_p.at[r], recv_p.at[r]
        )

        def pair(n, total):
            p = table_s[0, n]
            y = yb[table_s[1, n]]
            keep = table_s[2, n].astype(F32)
            both = dot_nt(y, wh[p])
            low = dot_nt(y[0:hours], wl[p])
            total = keep * total + (both[0:hours] + both[hours:] + low)
            seg[n] = total
            return total

        unrolled(0, pairs, 15, pair, jnp.zeros((hours, LANES), F32))

        def gradient(c, _):
            grad[c] = unit_v[c] - table_s[4, c].astype(F32) * seg[table_s[3, c]]
            return 0

        unrolled(0, cb, 5, gradient, 0)
        nb_src[4 + r] = grad[0, hours - 1 : hours, :]
        to_next(4 + r, r, 1)

        next_wait(1 + r)
        following = pltpu.roll(ys[rows_of(0), :], hours - 1, 0)
        following = jnp.where(row == hours - 1, nb_dst[1 + r] * has_after, following)
        grad[0] = grad[0] + following

        total = tm_sum(it)
        col_sums = total[:, 0:LANES]
        region_sums = total[:, LANES : 2 * LANES] + cap_change
        mr[r] = region_sums
        region_send(
            lambda k: mr.at[r], lambda k: sbuf.at[r, k - 1], send_r.at[r], recv_r.at[r]
        )
        capacity_grad = couple * dot_nt(
            jnp.broadcast_to(col_sums, (8, LANES)), sel_t, precision=HIGHEST
        )[0:1]

        pltpu.make_async_copy(rbuf.at[r], rbuf.at[r], recv_p.at[r]).wait()
        line_back = pbuf[r, 0]
        for k in range(nr - 1):
            line_back = line_back + rbuf[r, k]
        flow_grad = grad[3] - line_back
        grad[3] = flow_grad
        gat[r, me_r] = flow_grad
        region_send(
            lambda k: gat.at[r, me_r],
            lambda k: gat.at[r, me_r],
            send_g.at[it],
            recv_g.at[it],
        )
        next_wait(4 + r)
        prev_grad = nb_dst[4 + r] + ys[0:1, :]

        pltpu.make_async_copy(sbuf.at[r], sbuf.at[r], recv_r.at[r]).wait()
        sums = tree([mr[r]] + [sbuf[r, k] for k in range(nr - 1)])
        total_p = jnp.sum(jnp.where(lane_low, sums, 0.0), axis=1, keepdims=True)
        total_d = jnp.sum(jnp.where(lane_low, 0.0, sums), axis=1, keepdims=True)
        total_p = jnp.broadcast_to(total_p, (1, LANES))
        total_d = jnp.broadcast_to(total_d, (1, LANES))
        weight = jnp.sqrt(
            weight
            * jnp.sqrt(total_p / primal_count + EPSILON)
            / jnp.sqrt(total_d / dual_count + EPSILON)
        )
        primal_step = STEP_SCALE / weight
        dual_step = STEP_SCALE * weight

        def primal(c, a):
            bar, sq = primal_block(c, xs[rows_of(c), :], grad[c], primal_step)
            return bar, a + fold(sq)

        bar0, sq_p = primal(0, zero8)
        sq_p = unrolled(1, cb, 12, lambda c, a: primal(c, a)[1], sq_p)
        new_cap = jnp.maximum(cap - primal_step * (build - capacity_grad), 0.0)
        cap_diff = new_cap - cap
        prev_new = jnp.maximum(prev_x - primal_step * prev_grad, 0.0)
        prev_bar = prev_new + (prev_new - prev_x)

        def flow():
            pltpu.make_async_copy(
                gat.at[r, pl.ds(0, nr - 1)], gat.at[r, pl.ds(0, nr - 1)], recv_g.at[it]
            ).wait()
            line_grad = line_apply(lambda q: gat[r, q])
            new_line = line_a[...] - primal_step * line_grad
            line_a[...] = new_line
            return new_line - primal_step * line_grad

        sq_p = halves(sq_p)
        cap_change = jnp.where(lane_low, halves(cap_diff * cap_diff), 0.0)
        sq_d, col_own = forward(bar0, prev_bar, lambda: new_cap + cap_diff, flow, dual_step, False)
        return prev_new, new_cap, cap_change, weight, sq_p, sq_d, col_own

    first_diff = cap_new - cap_old
    carry = (
        prev_new,
        cap_new,
        jnp.where(lane_low, halves(first_diff * first_diff), 0.0),
        jnp.ones((1, LANES), F32),
        sq_p,
        sq_d,
        col_own,
    )
    carry = lax.fori_loop(1, ITERS, later, carry)
    cap_out[...] = pltpu.roll(carry[1], lax.rem(LANES - me_t * own_n, LANES), 1)

    for r in range(ITERS):
        pltpu.make_async_copy(tbuf.at[r], tbuf.at[r], send_t.at[r]).wait()
    pltpu.make_async_copy(
        gat0.at[pl.ds(0, nr - 1)], gat0.at[pl.ds(0, nr - 1)], send_g.at[0]
    ).wait()
    for r in range(ITERS - 1):
        pltpu.make_async_copy(sbuf.at[r], sbuf.at[r], send_r.at[r]).wait()
        pltpu.make_async_copy(rbuf.at[r], rbuf.at[r], send_p.at[r]).wait()
        pltpu.make_async_copy(
            gat.at[r, pl.ds(0, nr - 1)], gat.at[r, pl.ds(0, nr - 1)], send_g.at[r + 1]
        ).wait()
    for n in range(1 + 2 * (ITERS - 1)):
        pltpu.make_async_copy(nb_src.at[n], nb_src.at[n], send_n.at[n]).wait()


def to_results(x, y, cap, own):
    rows = x.shape[0]
    pieces = 4

    def place(x_ref, y_ref, cap_ref, x_out, y_out, cap_out, sem):
        copies = []
        for n in range(pieces):
            at = pl.ds(n * (rows // pieces), rows // pieces)
            copies.append(pltpu.make_async_copy(x_ref.at[at], x_out.at[at], sem.at[0, n]))
            copies.append(pltpu.make_async_copy(y_ref.at[at], y_out.at[at], sem.at[1, n]))
        for copy in copies:
            copy.start()
        cap_out[...] = cap_ref[:, 0:own]
        for copy in copies:
            copy.wait()

    vmem = pl.BlockSpec(memory_space=pltpu.VMEM)
    hbm = pl.BlockSpec(memory_space=pl.ANY)
    shape = jax.ShapeDtypeStruct(x.shape, F32)
    return pl.pallas_call(
        place,
        in_specs=[vmem, vmem, vmem],
        out_specs=(hbm, hbm, vmem),
        out_shape=(shape, shape, jax.ShapeDtypeStruct((1, own), F32)),
        scratch_shapes=[pltpu.SemaphoreType.DMA((2, pieces))],
        compiler_params=pltpu.CompilerParams(vmem_limit_bytes=8 * 2**20),
    )(x, y, cap)


def in_hbm(value):
    return pltpu.with_memory_space_constraint(value, pltpu.HBM)


def body(
    start_primal,
    demand,
    unit_cost,
    build_cost,
    start_capacity,
    net_weights,
    net_columns,
    line_weights,
    line_source,
    generator_map,
):
    hours, _, width = start_primal.shape
    bs = net_weights.shape[3]
    cb = width // bs
    s_count = net_weights.shape[2]
    nl = line_weights.shape[1]
    nt = lax.axis_size("tm")
    nr = lax.axis_size("region")
    pairs = cb * s_count
    sizes = (hours, cb, bs, s_count, nl, nt, nr)
    vmem = pl.BlockSpec(memory_space=pltpu.VMEM)
    hbm = pl.BlockSpec(memory_space=pltpu.HBM)
    rounds = ITERS - 1
    dma = pltpu.SemaphoreType.DMA
    x_new, y_new, cap = pl.pallas_call(
        functools.partial(kernel, sizes),
        out_shape=(
            jax.ShapeDtypeStruct((hours * cb, bs), F32),
            jax.ShapeDtypeStruct((hours * cb, bs), F32),
            jax.ShapeDtypeStruct((1, LANES), F32),
        ),
        in_specs=[hbm] * 10,
        out_specs=(vmem, vmem, vmem),
        scratch_shapes=[
            pltpu.SMEM((s_count, 1, cb), jnp.int32),
            pltpu.SMEM(line_source.shape[::-1], jnp.int32),
            pltpu.SMEM(start_capacity.shape, F32),
            pltpu.SMEM(build_cost.shape, F32),
            pltpu.VMEM(generator_map.shape, jnp.int32),
            pltpu.VMEM((cb, 1, bs), F32),
            pltpu.VMEM((hours * cb, bs), F32),
            pltpu.VMEM((hours * cb, bs), F32),
            pltpu.VMEM((cb, s_count, bs, bs), F32),
            pltpu.VMEM((nl * bs, bs), F32),
            pltpu.VMEM((nl * bs, bs), BF16),
            pltpu.VMEM((nl * bs, bs), BF16),
            pltpu.VMEM((pairs, bs, bs), BF16),
            pltpu.VMEM((pairs, bs, bs), BF16),
            pltpu.VMEM((cb, hours, bs), F32),
            pltpu.VMEM((cb, hours, bs), F32),
            pltpu.VMEM((cb, 2 * hours, bs), BF16),
            pltpu.VMEM((cb, 2 * hours, bs), BF16),
            pltpu.VMEM((pairs, hours, bs), F32),
            pltpu.VMEM((3, hours, bs), F32),
            pltpu.VMEM((8, LANES), jnp.int32),
            pltpu.SMEM((8, LANES), jnp.int32),
            pltpu.VMEM((1, LANES), jnp.int32),
            pltpu.SMEM((1, LANES), jnp.int32),
            pltpu.VMEM((hours, bs), F32),
            pltpu.VMEM((8, bs), F32),
            pltpu.VMEM((hours + 8, bs), F32),
            pltpu.VMEM((nr, hours + 8, bs), F32),
            pltpu.VMEM((rounds, nr, hours, bs), F32),
            pltpu.VMEM((rounds, nr, hours, bs), F32),
            pltpu.VMEM((rounds, nr - 1, hours, bs), F32),
            pltpu.VMEM((ITERS, 1, 2 * LANES), F32),
            pltpu.VMEM((ITERS, nt - 1, 1, 2 * LANES), F32),
            pltpu.VMEM((rounds, 1, LANES), F32),
            pltpu.VMEM((rounds, nr - 1, 1, LANES), F32),
            pltpu.VMEM((1 + 2 * rounds, 1, LANES), F32),
            pltpu.VMEM((1 + 2 * rounds, 1, LANES), F32),
            dma((11,)),
            dma((cb // 5 if cb % 5 == 0 else cb,)),
            dma((ITERS,)),
            dma((ITERS,)),
            dma((rounds,)),
            dma((rounds,)),
            dma((ITERS,)),
            dma((ITERS,)),
            dma((rounds,)),
            dma((rounds,)),
            dma((1 + 2 * rounds,)),
            dma((1 + 2 * rounds,)),
        ],
        compiler_params=pltpu.CompilerParams(
            collective_id=0, has_side_effects=True, vmem_limit_bytes=40 * 2**20
        ),
    )(*(in_hbm(v) for v in (
        jnp.transpose(net_columns, (2, 0, 1)),
        jnp.transpose(line_source),
        start_capacity,
        build_cost,
        generator_map,
        unit_cost.reshape(cb, 1, bs),
        start_primal.reshape(hours * cb, bs),
        demand.reshape(hours * cb, bs),
        net_weights[0],
        line_weights.reshape(nl * bs, bs),
    )))
    x_new, y_new, capacity = to_results(x_new, y_new, cap, start_capacity.shape[1])
    return x_new.reshape(hours, 1, width), y_new.reshape(hours, 1, width), capacity


def solution(mesh):
    in_specs = (
        P("tm", "region", None),
        P("tm", "region", None),
        P("region", None),
        P("region", "tm"),
        P("region", "tm"),
        P("region", None, None, None, None),
        P("region", None, None),
        P("region", None, None, None),
        P(),
        P("region", None),
    )
    out_specs = (P("tm", "region", None), P("tm", "region", None), P("region", "tm"))
    return jax.shard_map(body, mesh=mesh, in_specs=in_specs, out_specs=out_specs, check_vma=False)
```
